32 devices in a mesh: row: 16 (over z, y, x), col: 2 (over core).
Axes of the slice: x: 2, y: 2, z: 4, core: 2. Of those that a mesh axis runs over, the one named last changes fastest.
Arguments:
- noise: bfloat16 [8, 2, 16, 2048], P(None, None, 'row', 'col'), may hold values from -6 to 6
- diag_factor: bfloat16 [2, 16, 2048, 2048], P(None, 'row', 'col'), may hold values from -0.125 to 0.125
- left_factor: bfloat16 [16, 32, 64, 2048], P('row', None, None, 'col'), may hold values from -0.125 to 0.125
- right_factor: bfloat16 [16, 32, 64, 2048], P('row', None, None, 'col'), may hold values from -0.125 to 0.125
- tile_ranks: int32 [16, 32], P('row'), may hold values from 1 to 64
- pair_first: int32 [16, 2, 4096], P('row', 'col'), may hold values from 4096 to 8191
- pair_partner: int32 [16, 2, 4096], P('row', 'col'), may hold values from 0 to 8191, as said below
- bin_ids: int32 [16, 2, 4096], P('row', 'col'), may hold values from 0 to 127, as said below
Outputs:
- samples: float32 [8, 2, 16, 2048], P(None, None, 'row', 'col')
- variogram: float32 [8, 128], replicated
The draws below stay inside these ranges and needn't reach their ends.
Inputs may be any that keep to these rules, and one draw needn't show every extreme that they name: Pairs of the first tile-row pair (r = 0) have pair_partner of 4096 or more. `bin_ids`: bins may hold no pair.
All inputs are finite; a program needn't handle non-finite values.
Results may differ from the reference program's by a relative error of at most 0.0012.
Values may be sent and summed in bfloat16 or wider, within the bound.
A program may use at most 64 MiB of HBM per device.

```python
import jax
import jax.numpy as jnp
from jax import lax

SAMPLES = 8
TILE = 2048
RMAX = 64
NBIN = 128
PAIRS = 4096
NT = 32
N_ROW = 16
N_COL = 2


def draw_pair_partner(key, part):
    first_row = jnp.arange(N_ROW, dtype=jnp.int32) == 0
    lowest = jnp.where(first_row, 2 * TILE, 0).astype(jnp.int32)[:, None, None]
    return jax.random.randint(key, (N_ROW, N_COL, PAIRS), lowest, 4 * TILE, dtype=jnp.int32)


def draw_bin_ids(key, part):
    order_key = jax.random.fold_in(key, 101)
    choose_key = jax.random.fold_in(key, 202)
    bin_order = jax.random.permutation(order_key, NBIN).astype(jnp.int32)
    live_count = NBIN - max(1, NBIN // 8)
    pick_index = jax.random.randint(choose_key, (N_ROW, N_COL, PAIRS), 0, live_count, dtype=jnp.int32)
    return jnp.take(bin_order, pick_index).astype(jnp.int32)


def set_ends(drawn, own_key, least, largest):
    extent = drawn.shape
    spot = [jax.random.randint(jax.random.fold_in(own_key, axis), (), 0, extent[axis]) for axis in range(len(extent))]
    drawn = drawn.at[tuple(spot)].set(least)
    longest = extent.index(max(extent))
    spot[longest] = (spot[longest] + 1) % extent[longest]
    return drawn.at[tuple(spot)].set(largest)


def block_scale(rng, extent, split, smallest, largest):
    def one(position, parts):
        heights = jax.random.uniform(jax.random.fold_in(jax.random.fold_in(rng, 6), position), (parts,), jnp.float32, smallest / len(split), largest / len(split))
        return jnp.repeat(jnp.exp(heights), extent[position] // parts).reshape((-1,) + (1,) * (len(extent) - position - 1))

    level = one(*split[0])
    for cut in split[1:]:
        level = level * one(*cut)
    return level


def normal_values(rng, extent, spread, limit, pieces=(), kind=jnp.bfloat16):
    factor_of = block_scale(rng, extent, pieces, -0.22, 0.18) if pieces else 1.0
    array = jax.random.normal(rng, extent, jnp.float32) * spread * factor_of
    return jnp.minimum(jnp.maximum(array, -limit), limit).astype(kind)


def setup_inputs(seed: int = 0) -> dict:
    key_of = jax.random.split(jax.random.key(seed), 9)
    return {
        "noise": normal_values(key_of[0], (SAMPLES, 2, N_ROW, TILE), 1.0, 6.0, ((2, 16), (3, 2))),
        "diag_factor": normal_values(key_of[1], (2, N_ROW, TILE, TILE), TILE ** -0.5, 0.125, ((1, 16), (2, 2))),
        "left_factor": normal_values(key_of[2], (N_ROW, NT, RMAX, TILE), (RMAX * NT) ** -0.5, 0.125, ((0, 16), (3, 2))),
        "right_factor": normal_values(key_of[3], (N_ROW, NT, RMAX, TILE), TILE ** -0.5, 0.125, ((0, 16), (3, 2))),
        "tile_ranks": set_ends(jax.random.randint(key_of[4], (N_ROW, NT), 1, RMAX + 1), jax.random.fold_in(key_of[4], 1), 1, RMAX).astype(jnp.int32),
        "pair_first": set_ends(jax.random.randint(key_of[5], (N_ROW, N_COL, PAIRS), 2 * TILE, 4 * TILE), jax.random.fold_in(key_of[5], 1), 2 * TILE, (4 * TILE) - 1).astype(jnp.int32),
        "pair_partner": draw_pair_partner(jax.random.fold_in(key_of[8], 71), 0),
        "bin_ids": draw_bin_ids(jax.random.fold_in(key_of[8], 71), 0),
    }


def reference(noise, diag_factor, left_factor, right_factor, tile_ranks, pair_first, pair_partner, bin_ids):
    tile_count = 2 * N_ROW
    ordered = jnp.concatenate([noise[:, 0], noise[:, 1][:, ::-1]], axis=1)
    idx_tile = jnp.arange(TILE, dtype=jnp.int32)
    below = idx_tile[None, :] < idx_tile[:, None]
    ident = (idx_tile[None, :] == idx_tile[:, None]).astype(jnp.float32)
    slot_ids = jnp.arange(tile_count, dtype=jnp.int32)
    rank_ids = jnp.arange(RMAX, dtype=jnp.int32)

    def one_pair(pair_id):
        tiles_diag = diag_factor[:, pair_id].astype(jnp.float32)
        effective = jnp.where(below[None], tiles_diag, 0.0) + ident[None]
        own_noise = jnp.stack([ordered[:, pair_id], ordered[:, tile_count - 1 - pair_id]], axis=1).astype(jnp.float32)
        on_diag = jnp.einsum('sht,hit->shi', own_noise, effective, precision=lax.Precision.HIGHEST)
        source = jnp.where(slot_ids < pair_id, slot_ids, slot_ids - pair_id).astype(jnp.int32)
        chosen = jnp.take(ordered, source, axis=1).astype(jnp.float32)
        projected = jnp.einsum('skt,kqt->ksq', chosen, right_factor[pair_id].astype(jnp.float32), precision=lax.Precision.HIGHEST)
        in_rank = rank_ids[None, :] < tile_ranks[pair_id][:, None]
        coeffs = jnp.where(in_rank[:, None, :], projected, 0.0).astype(jnp.bfloat16)
        coeffs = lax.optimization_barrier(coeffs).astype(jnp.float32)
        select = jnp.stack([slot_ids < pair_id, (slot_ids >= pair_id) & (slot_ids < tile_count - 1)]).astype(jnp.float32)
        weighted = select[:, :, None, None] * coeffs[None]
        off_diag = jnp.einsum('hksq,kqt->sht', weighted, left_factor[pair_id].astype(jnp.float32), precision=lax.Precision.HIGHEST)
        return on_diag + off_diag

    stacked = lax.map(one_pair, jnp.arange(N_ROW, dtype=jnp.int32))
    samples = jnp.transpose(stacked, (1, 2, 0, 3))
    previous = jnp.concatenate([jnp.zeros_like(samples[:, :, :1]), samples[:, :, :-1]], axis=2)
    pooled = jnp.concatenate([previous[:, 0], previous[:, 1], samples[:, 0], samples[:, 1]], axis=-1)
    first_idx = pair_first.reshape(N_ROW, N_COL * PAIRS)
    second_idx = pair_partner.reshape(N_ROW, N_COL * PAIRS)
    first_val = jnp.take_along_axis(pooled, first_idx[None], axis=2)
    second_val = jnp.take_along_axis(pooled, second_idx[None], axis=2)
    differ = first_val - second_val
    half_sq = 0.5 * differ * differ
    half_sq = jnp.transpose(half_sq.reshape(SAMPLES, N_ROW * N_COL, PAIRS), (1, 0, 2))
    bin_blocks = bin_ids.reshape(N_ROW * N_COL, PAIRS)
    bin_range = jnp.arange(NBIN, dtype=jnp.int32)

    def add_block(carry, items):
        block_sq, block_bins = items
        onehot = (block_bins[:, None] == bin_range[None, :]).astype(jnp.float32)
        sums = carry[0] + jnp.dot(block_sq, onehot, precision=lax.Precision.HIGHEST, preferred_element_type=jnp.float32)
        counts = carry[1] + jnp.sum(onehot, axis=0)
        return (sums, counts), None

    start = (jnp.zeros((SAMPLES, NBIN), jnp.float32), jnp.zeros((NBIN,), jnp.float32))
    (bin_sums, bin_counts), _ = lax.scan(add_block, start, (half_sq, bin_blocks))
    variogram = bin_sums / jnp.maximum(bin_counts, 1.0)[None, :]
    return samples, variogram
```

```python
import functools

import jax
import jax.numpy as jnp
from jax import lax
from jax.experimental import pallas as pl
from jax.experimental.pallas import tpu as pltpu
from jax.sharding import PartitionSpec as P

NBIN = 128
LANES = 128
PLANE = 4
MESH = pl.DeviceIdType.MESH
NT_DIMS = (((1,), (1,)), ((), ()))


def kernel(
    dims,
    z_ref, diag_ref, left_ref, right_ref, ranks_ref, first_ref, second_ref, bins_ref,
    samples_ref, vario_ref,
    zbuf, zpeer, down, doff, vbuf, ubuf, proj, acc, full, sbf, prev, prev32, diff, red1, red2, red3,
    own_sem, off_sem, v_sem, u_sem,
    z_send, z_recv, zp_send, zp_recv, pj_send, pj_recv, sm_send, sm_recv, pv_send, pv_recv,
    r1_send, r1_recv, r2_send, r2_recv, r3_send, r3_recv,
):
    rows, cols, count, shard, tile, rank, strip = dims
    layers = rows // PLANE
    tiles = 2 * rows
    r = lax.axis_index("row")
    c = lax.axis_index("col")
    b = lax.rem(r, PLANE)
    a = lax.div(r, PLANE)
    x_at = lax.rem(r, 2)
    y_at = lax.div(b, 2)
    x_step = 1 - 2 * x_at
    y_step = 2 - 4 * y_at
    strips = shard // strip
    pending = []

    def remote(src, dst, send, recv, row, col):
        return pltpu.make_async_remote_copy(
            src_ref=src, dst_ref=dst, send_sem=send, recv_sem=recv,
            device_id=(row, col), device_id_type=MESH,
        )

    def push(*args):
        copy = remote(*args)
        copy.start()
        pending.append(copy)

    own_copies = {}
    off_copies = {}
    for h in range(2):
        for s in range(strips):
            width = (s + 1) * strip
            own_copies[h, s] = pltpu.make_async_copy(
                diag_ref.at[h, pl.ds(s * strip, strip), pl.ds(pl.multiple_of(c * shard, LANES), width)],
                down.at[h, pl.ds(s * strip, strip), pl.ds(0, width)],
                own_sem.at[h, s],
            )
            own_copies[h, s].start()
    for h in range(2):
        for d in range(1, cols):
            at = jnp.maximum(c - d, 0)
            off_copies[h, d] = pltpu.make_async_copy(
                diag_ref.at[h, :, pl.ds(pl.multiple_of(at * shard, LANES), shard)],
                doff.at[h, d - 1],
                off_sem.at[h, d - 1],
            )

            @pl.when(c >= d)
            def _(copy=off_copies[h, d]):
                copy.start()

    v_parts = v_sem.shape[0]
    part = tiles * rank // v_parts
    v_copies = [
        pltpu.make_async_copy(right_ref.at[pl.ds(i * part, part)], vbuf.at[pl.ds(i * part, part)], v_sem.at[i])
        for i in range(v_parts)
    ]
    u_copies = [
        pltpu.make_async_copy(left_ref.at[pl.ds(i * part, part)], ubuf.at[pl.ds(i * part, part)], u_sem.at[i])
        for i in range(v_parts)
    ]
    for copy in v_copies + u_copies:
        copy.start()

    barrier = pltpu.get_barrier_semaphore()

    def greet(row, col):
        pl.semaphore_signal(barrier, inc=1, device_id=(row, col), device_id_type=MESH)

    col_peers = [lax.rem(c + d, cols) for d in range(1, cols)]
    plane_peers = [a * PLANE + lax.rem(b + d, PLANE) for d in range(1, PLANE)]
    layer_peers = [lax.rem(a + d, layers) * PLANE + b for d in range(1, layers)]
    for peer in layer_peers + plane_peers:
        greet(peer, c)
    for peer in col_peers:
        greet(r, peer)

    @pl.when(r < rows - 1)
    def _():
        for k in range(cols):
            greet(r + 1, k)

    @pl.when(r > 0)
    def _():
        for k in range(cols):
            greet(r - 1, k)

    expected = (cols - 1) + (PLANE - 1) + (layers - 1)
    expected = expected + jnp.where(r < rows - 1, cols, 0) + jnp.where(r > 0, cols, 0)
    pl.semaphore_wait(barrier, expected)

    def tile_of(owner, h):
        return owner if h == 0 else tiles - 1 - owner

    send_at = [0]

    def z_push(src, owner, h, row):
        j = tile_of(owner, h)
        push(src, zbuf.at[j], z_send.at[send_at[0]], z_recv.at[j], row, c)
        send_at[0] += 1

    def z_wait(owner, h):
        j = tile_of(owner, h)
        remote(zbuf.at[j], zbuf.at[j], z_send.at[0], z_recv.at[j], r, c).wait_recv()

    row_x = r + x_step
    row_y = r + y_step
    near = (row_y, row_x)
    far = (row_x, row_y)
    for peer in layer_peers:
        for h in range(2):
            z_push(z_ref.at[h], r, h, peer)
    for h in range(2):
        z_push(z_ref.at[h], r, h, near[h])
        z_push(z_ref.at[h], r, h, far[h])
    for i, peer in enumerate(col_peers):
        push(z_ref, zpeer.at[c], zp_send.at[i], zp_recv.at[c], r, peer)
    for h in range(2):
        zbuf[tile_of(r, h)] = z_ref[h]

    def diag_chunk(h, s):
        own_copies[h, s].wait()
        lanes = pl.ds(s * strip, strip)
        block = down[h, lanes, lanes]
        below = (
            lax.broadcasted_iota(jnp.int32, (strip, strip), 1)
            < lax.broadcasted_iota(jnp.int32, (strip, strip), 0)
        )
        block = jnp.where(below, block.astype(jnp.float32), 0.0).astype(jnp.bfloat16)
        mine = z_ref[h, :, lanes]
        value = mine.astype(jnp.float32)
        value += lax.dot_general(mine, block, NT_DIMS, preferred_element_type=jnp.float32)
        if s:
            value += lax.dot_general(
                z_ref[h, :, : s * strip], down[h, lanes, : s * strip], NT_DIMS,
                preferred_element_type=jnp.float32,
            )
        acc[h * count : (h + 1) * count, lanes] = value

    def off_chunk(h, d):
        @pl.when(c >= d)
        def _():
            off_copies[h, d].wait()
            at = jnp.maximum(c - d, 0)
            acc[h * count : (h + 1) * count, :] += lax.dot_general(
                zpeer[at, h], doff[h, d - 1], NT_DIMS, preferred_element_type=jnp.float32
            )

    work = [functools.partial(diag_chunk, h, s) for h in range(2) for s in range(strips)]
    spare = [functools.partial(off_chunk, h, d) for h in range(2) for d in range(1, cols)]

    def some(n):
        for _ in range(n):
            if work:
                work.pop(0)()

    some(strips)
    layer_owner = [lax.rem(a + d, layers) * PLANE + b for d in range(1, layers)]
    for owner in layer_owner:
        for h in range(2):
            z_wait(owner, h)
            j = tile_of(owner, h)
            z_push(zbuf.at[j], owner, h, near[h])
            z_push(zbuf.at[j], owner, h, far[h])
        some(1)
    some(len(work))
    for i, peer in enumerate(col_peers):
        remote(z_ref, zpeer.at[peer], zp_send.at[i], zp_recv.at[peer], r, peer).wait_recv()
    second_step = (y_step, x_step)
    for owner in [r] + layer_owner:
        for h in range(2):
            from_near = owner + second_step[h]
            z_wait(from_near, h)
            j = tile_of(from_near, h)
            z_push(zbuf.at[j], from_near, h, far[h])
        if spare:
            spare.pop(0)()
    while spare:
        spare.pop(0)()
    last_step = (x_step, y_step)
    for owner in [r] + layer_owner:
        for h in range(2):
            z_wait(owner + last_step[h], h)
            z_wait(owner + x_step + y_step, h)

    group = 256 // rank
    lane_slot = lax.div(lax.broadcasted_iota(jnp.int32, (count, group * rank), 1), rank)
    lane_rank = lax.rem(lax.broadcasted_iota(jnp.int32, (count, group * rank), 1), rank)
    waited = 0
    for g in range(tiles // group):
        while waited * part < (g + 1) * group * rank:
            v_copies[waited].wait()
            waited += 1
        chosen = []
        for i in range(group):
            k = g * group + i
            chosen.append(zbuf[jnp.where(k < r, k, jnp.maximum(k - r, 0))].astype(jnp.float32))
        lhs = jnp.concatenate(chosen, axis=0).astype(jnp.bfloat16)
        span = pl.ds(g * group * rank, group * rank)
        result = lax.dot_general(lhs, vbuf[span, :], NT_DIMS, preferred_element_type=jnp.float32)
        value = result[:count]
        for i in range(1, group):
            value = jnp.where(lane_slot == i, result[i * count : (i + 1) * count], value)
        proj[c, :, span] = value
    for i, peer in enumerate(col_peers):
        push(proj.at[c], proj.at[c], pj_send.at[i], pj_recv.at[c], r, peer)
    for copy in u_copies:
        copy.wait()
    for i, peer in enumerate(col_peers):
        remote(proj.at[c], proj.at[peer], pj_send.at[i], pj_recv.at[peer], r, peer).wait_recv()
    weighted = []
    for g in range(tiles // group):
        span = pl.ds(g * group * rank, group * rank)
        value = proj[0, :, span]
        for k in range(1, cols):
            value = value + proj[k, :, span]
        limit = jnp.zeros((count, group * rank), jnp.int32)
        for i in range(group):
            limit = jnp.where(lane_slot == i, ranks_ref[0, g * group + i], limit)
        value = jnp.where(lane_rank < limit, value, 0.0)
        slot = lane_slot + g * group
        weighted.append(
            jnp.concatenate(
                [
                    jnp.where(slot < r, value, 0.0),
                    jnp.where((slot >= r) & (slot < tiles - 1), value, 0.0),
                ],
                axis=0,
            ).astype(jnp.bfloat16)
        )
    weights = jnp.concatenate(weighted, axis=1)
    value = acc[...] + jnp.dot(weights, ubuf[...], preferred_element_type=jnp.float32)
    full[c] = value
    sbf[...] = value.astype(jnp.bfloat16)
    for i, peer in enumerate(col_peers):
        push(full.at[c], full.at[c], sm_send.at[i], sm_recv.at[c], r, peer)
    prev_copies = [
        remote(sbf, prev.at[c], pv_send.at[k], pv_recv.at[c], jnp.minimum(r + 1, rows - 1), k)
        for k in range(cols)
    ]

    @pl.when(r < rows - 1)
    def _():
        for copy in prev_copies:
            copy.start()

    for h in range(2):
        samples_ref[h] = value[h * count : (h + 1) * count]
    for i, peer in enumerate(col_peers):
        remote(full.at[c], full.at[peer], sm_send.at[i], sm_recv.at[peer], r, peer).wait_recv()

    groups = first_ref.shape[0]
    per_row = shard // LANES
    own_first = 2 * tile // LANES
    batch = 4

    def table(ref, h, j):
        return ref[j // per_row, h * count : (h + 1) * count, (j % per_row) * LANES : (j % per_row + 1) * LANES]

    def split(ref, at):
        index = jnp.broadcast_to(ref[pl.ds(at, 1), :], (count, LANES))
        return lax.shift_right_logical(index, 7), lax.bitwise_and(index, LANES - 1)

    def pick(entry, low):
        return jnp.take_along_axis(entry, low, axis=1, mode="promise_in_bounds")

    def own_part(step, carry):
        ats = [step * batch + i for i in range(batch)]
        one = [split(first_ref, at) for at in ats]
        two = [split(second_ref, at) for at in ats]
        got_one = [jnp.zeros((count, LANES), jnp.float32) for _ in ats]
        got_two = [jnp.zeros((count, LANES), jnp.float32) for _ in ats]
        for h in range(2):
            for j in range(tile // LANES):
                entry = table(full, h, j)
                number = own_first + h * (tile // LANES) + j
                for i in range(batch):
                    got_one[i] = jnp.where(one[i][0] == number, pick(entry, one[i][1]), got_one[i])
                    got_two[i] = jnp.where(two[i][0] == number, pick(entry, two[i][1]), got_two[i])
        for i in range(batch):
            diff[ats[i]] = got_one[i] - got_two[i]
        return carry

    lax.fori_loop(0, groups // batch, own_part, 0)

    @pl.when(r > 0)
    def _():
        for k in range(cols):
            remote(sbf, prev.at[k], pv_send.at[k], pv_recv.at[k], r, c).wait_recv()
        prev32[...] = prev[...].astype(jnp.float32)

    @pl.when(r == 0)
    def _():
        prev32[...] = jnp.zeros_like(prev32)

    bin_rows = lax.broadcasted_iota(jnp.int32, (NBIN, LANES), 0)

    def prev_part(step, sums):
        ats = [step * batch + i for i in range(batch)]
        two = [split(second_ref, at) for at in ats]
        got = [jnp.zeros((count, LANES), jnp.float32) for _ in ats]
        for h in range(2):
            for j in range(tile // LANES):
                entry = table(prev32, h, j)
                number = h * (tile // LANES) + j
                for i in range(batch):
                    got[i] = jnp.where(two[i][0] == number, pick(entry, two[i][1]), got[i])
        for i in range(batch):
            differ = diff[ats[i]] - got[i]
            half_sq = 0.5 * differ * differ
            high = half_sq.astype(jnp.bfloat16).astype(jnp.float32)
            terms = jnp.concatenate(
                [high, half_sq - high, jnp.ones((count, LANES), jnp.float32)], axis=0
            ).astype(jnp.bfloat16)
            onehot = jnp.where(
                jnp.broadcast_to(bins_ref[pl.ds(ats[i], 1), :], (NBIN, LANES)) == bin_rows, 1.0, 0.0
            ).astype(jnp.bfloat16)
            sums = sums + lax.dot_general(terms, onehot, NT_DIMS, preferred_element_type=jnp.float32)
        return sums

    sums = lax.fori_loop(0, groups // batch, prev_part, jnp.zeros((3 * count, NBIN), jnp.float32))
    total = jnp.concatenate([sums[:count] + sums[count : 2 * count], sums[2 * count :]], axis=0)

    def reduce_stage(value, buf, at, peers, send, recv, number):
        buf[at] = value
        for i, (row, col, slot) in enumerate(peers):
            push(buf.at[at], buf.at[at], send.at[i], recv.at[at], row, col)
        for i, (row, col, slot) in enumerate(peers):
            remote(buf.at[at], buf.at[slot], send.at[i], recv.at[slot], row, col).wait_recv()
        out = buf[0]
        for i in range(1, number):
            out = out + buf[i]
        return out

    total = reduce_stage(total, red1, c, [(r, p, p) for p in col_peers], r1_send, r1_recv, cols)
    total = reduce_stage(
        total, red2, b, [(p, c, lax.rem(p, PLANE)) for p in plane_peers], r2_send, r2_recv, PLANE
    )
    total = reduce_stage(
        total, red3, a, [(p, c, lax.div(p, PLANE)) for p in layer_peers], r3_send, r3_recv, layers
    )
    vario_ref[...] = total[:count] / jnp.maximum(total[count:], 1.0)

    for copy in pending:
        copy.wait_send()

    @pl.when(r < rows - 1)
    def _():
        for copy in prev_copies:
            copy.wait_send()


def body(
    noise, diag_factor, left_factor, right_factor, tile_ranks, pair_first, pair_partner, bin_ids
):
    rows = lax.axis_size("row")
    cols = lax.axis_size("col")
    count = noise.shape[0]
    shard = noise.shape[3]
    tile = shard * cols
    tiles = 2 * rows
    rank = right_factor.shape[2]
    strip = min(256, shard)
    layers = rows // PLANE
    v_parts = 4
    z = jnp.transpose(noise[:, :, 0], (1, 0, 2))
    dma = lambda *shape: pltpu.SemaphoreType.DMA(shape)
    vmem = pl.BlockSpec(memory_space=pltpu.VMEM)
    hbm = pl.BlockSpec(memory_space=pl.ANY)
    smem = pl.BlockSpec(memory_space=pltpu.SMEM)
    off = max(cols - 1, 1)
    f32, bf16 = jnp.float32, jnp.bfloat16
    samples, vario = pl.pallas_call(
        functools.partial(kernel, (rows, cols, count, shard, tile, rank, strip)),
        out_shape=(
            jax.ShapeDtypeStruct((2, count, shard), f32),
            jax.ShapeDtypeStruct((count, NBIN), f32),
        ),
        in_specs=[vmem, hbm, hbm, hbm, smem, vmem, vmem, vmem],
        out_specs=(vmem, vmem),
        scratch_shapes=[
            pltpu.VMEM((tiles, count, shard), bf16),
            pltpu.VMEM((cols, 2, count, shard), bf16),
            pltpu.VMEM((2, shard, shard), bf16),
            pltpu.VMEM((2, off, shard, shard), bf16),
            pltpu.VMEM((tiles * rank, shard), bf16),
            pltpu.VMEM((tiles * rank, shard), bf16),
            pltpu.VMEM((cols, count, tiles * rank), f32),
            pltpu.VMEM((2 * count, shard), f32),
            pltpu.VMEM((cols, 2 * count, shard), f32),
            pltpu.VMEM((2 * count, shard), bf16),
            pltpu.VMEM((cols, 2 * count, shard), bf16),
            pltpu.VMEM((cols, 2 * count, shard), f32),
            pltpu.VMEM((pair_first.shape[2] // LANES, count, LANES), f32),
            pltpu.VMEM((cols, 2 * count, NBIN), f32),
            pltpu.VMEM((PLANE, 2 * count, NBIN), f32),
            pltpu.VMEM((layers, 2 * count, NBIN), f32),
            dma(2, shard // strip), dma(2, off), dma(v_parts), dma(v_parts),
            dma(2 * (layers - 1) + 6 * layers + 8), dma(tiles), dma(off), dma(cols),
            dma(off), dma(cols), dma(off), dma(cols), dma(cols), dma(cols),
            dma(off), dma(cols), dma(PLANE), dma(PLANE), dma(layers), dma(layers),
        ],
        compiler_params=pltpu.CompilerParams(collective_id=0, has_side_effects=True),
    )(
        z,
        diag_factor.reshape(2, shard, tile),
        left_factor.reshape(tiles * rank, shard),
        right_factor.reshape(tiles * rank, shard),
        tile_ranks,
        pair_first.reshape(-1, LANES),
        pair_partner.reshape(-1, LANES),
        bin_ids.reshape(-1, LANES),
    )
    return jnp.transpose(samples, (1, 0, 2))[:, :, None, :], vario


def solution(mesh):
    in_specs = (
        P(None, None, "row", "col"),
        P(None, "row", "col", None),
        P("row", None, None, "col"),
        P("row", None, None, "col"),
        P("row", None),
        P("row", "col", None),
        P("row", "col", None),
        P("row", "col", None),
    )
    out_specs = (P(None, None, "row", "col"), P())
    return jax.shard_map(body, mesh=mesh, in_specs=in_specs, out_specs=out_specs, check_vma=False)
```

```python
import functools

import jax
import jax.numpy as jnp
from jax import lax
from jax.experimental import pallas as pl
from jax.experimental.pallas import tpu as pltpu
from jax.sharding import PartitionSpec as P

NBIN = 128
LANES = 128
PLANE = 4
MESH = pl.DeviceIdType.MESH
NT_DIMS = (((1,), (1,)), ((), ()))


def kernel(
    dims,
    z_ref, diag_ref, left_ref, right_ref, ranks_ref, first_ref, second_ref, bins_ref,
    samples_ref, vario_ref,
    zbuf, zpeer, down, doff, vbuf, ubuf, proj, acc, full, sbf, prev, prev32, diff, red1, red2, red3,
    own_sem, off_sem, v_sem, u_sem,
    z_send, z_recv, zp_send, zp_recv, pj_send, pj_recv, sm_send, sm_recv, pv_send, pv_recv,
    r1_send, r1_recv, r2_send, r2_recv, r3_send, r3_recv,
):
    rows, cols, count, shard, tile, rank, strip = dims
    layers = rows // PLANE
    tiles = 2 * rows
    r = lax.axis_index("row")
    c = lax.axis_index("col")
    b = lax.rem(r, PLANE)
    a = lax.div(r, PLANE)
    x_at = lax.rem(r, 2)
    y_at = lax.div(b, 2)
    x_step = 1 - 2 * x_at
    y_step = 2 - 4 * y_at
    strips = shard // strip
    pending = []

    def remote(src, dst, send, recv, row, col):
        return pltpu.make_async_remote_copy(
            src_ref=src, dst_ref=dst, send_sem=send, recv_sem=recv,
            device_id=(row, col), device_id_type=MESH,
        )

    def push(*args):
        copy = remote(*args)
        copy.start()
        pending.append(copy)

    own_copies = {}
    off_copies = {}
    for h in range(2):
        for s in range(strips):
            width = (s + 1) * strip
            own_copies[h, s] = pltpu.make_async_copy(
                diag_ref.at[h, pl.ds(s * strip, strip), pl.ds(pl.multiple_of(c * shard, LANES), width)],
                down.at[h, pl.ds(s * strip, strip), pl.ds(0, width)],
                own_sem.at[h, s],
            )
            own_copies[h, s].start()
    for h in range(2):
        for d in range(1, cols):
            at = jnp.maximum(c - d, 0)
            off_copies[h, d] = pltpu.make_async_copy(
                diag_ref.at[h, :, pl.ds(pl.multiple_of(at * shard, LANES), shard)],
                doff.at[h, d - 1],
                off_sem.at[h, d - 1],
            )

            @pl.when(c >= d)
            def _(copy=off_copies[h, d]):
                copy.start()

    v_parts = v_sem.shape[0]
    part = tiles * rank // v_parts
    v_copies = [
        pltpu.make_async_copy(right_ref.at[pl.ds(i * part, part)], vbuf.at[pl.ds(i * part, part)], v_sem.at[i])
        for i in range(v_parts)
    ]
    u_copies = [
        pltpu.make_async_copy(left_ref.at[pl.ds(i * part, part)], ubuf.at[pl.ds(i * part, part)], u_sem.at[i])
        for i in range(v_parts)
    ]
    for copy in v_copies + u_copies:
        copy.start()

    barrier = pltpu.get_barrier_semaphore()

    def greet(row, col):
        pl.semaphore_signal(barrier, inc=1, device_id=(row, col), device_id_type=MESH)

    col_peers = [lax.rem(c + d, cols) for d in range(1, cols)]
    plane_peers = [a * PLANE + lax.rem(b + d, PLANE) for d in range(1, PLANE)]
    layer_peers = [lax.rem(a + d, layers) * PLANE + b for d in range(1, layers)]
    for peer in plane_peers:
        greet(peer, c)

    @pl.when(a < layers - 1)
    def _():
        greet(r + PLANE, c)

    @pl.when(a > 0)
    def _():
        greet(r - PLANE, c)

    for peer in col_peers:
        greet(r, peer)

    @pl.when(r < rows - 1)
    def _():
        for k in range(cols):
            greet(r + 1, k)

    @pl.when(r > 0)
    def _():
        for k in range(cols):
            greet(r - 1, k)

    expected = (cols - 1) + (PLANE - 1)
    expected = expected + jnp.where(a < layers - 1, 1, 0) + jnp.where(a > 0, 1, 0)
    expected = expected + jnp.where(r < rows - 1, cols, 0) + jnp.where(r > 0, cols, 0)
    pl.semaphore_wait(barrier, expected)

    def tile_of(owner, h):
        return owner if h == 0 else tiles - 1 - owner

    send_at = [0]
    guarded = []

    def z_push(src, owner, h, row, cond=None):
        j = tile_of(owner, h)
        copy = remote(src, zbuf.at[j], z_send.at[send_at[0]], z_recv.at[j], row, c)
        send_at[0] += 1
        if cond is None:
            copy.start()
            pending.append(copy)
        else:
            guarded.append((cond, copy))
            pl.when(cond)(copy.start)

    def z_wait(owner, h, cond=None):
        j = tile_of(owner, h)
        copy = remote(zbuf.at[j], zbuf.at[j], z_send.at[0], z_recv.at[j], r, c)
        if cond is None:
            copy.wait_recv()
        else:
            pl.when(cond)(copy.wait_recv)

    row_x = r + x_step
    row_y = r + y_step
    near = (row_y, row_x)
    far = (row_x, row_y)
    row_up = jnp.minimum(r + PLANE, rows - PLANE + b)
    row_down = jnp.maximum(r - PLANE, b)
    can_up = a < layers - 1
    can_down = a > 0
    z_push(z_ref.at[0], r, 0, row_down, can_down)
    z_push(z_ref.at[0], r, 0, row_up, can_up)
    z_push(z_ref.at[1], r, 1, row_down, can_down)
    for h in range(2):
        z_push(z_ref.at[h], r, h, near[h])
        z_push(z_ref.at[h], r, h, far[h])
    for i, peer in enumerate(col_peers):
        push(z_ref, zpeer.at[c], zp_send.at[i], zp_recv.at[c], r, peer)
    for h in range(2):
        zbuf[tile_of(r, h)] = z_ref[h]

    def diag_chunk(h, s):
        own_copies[h, s].wait()
        lanes = pl.ds(s * strip, strip)
        block = down[h, lanes, lanes]
        below = (
            lax.broadcasted_iota(jnp.int32, (strip, strip), 1)
            < lax.broadcasted_iota(jnp.int32, (strip, strip), 0)
        )
        block = jnp.where(below, block.astype(jnp.float32), 0.0).astype(jnp.bfloat16)
        mine = z_ref[h, :, lanes]
        value = mine.astype(jnp.float32)
        value += lax.dot_general(mine, block, NT_DIMS, preferred_element_type=jnp.float32)
        if s:
            value += lax.dot_general(
                z_ref[h, :, : s * strip], down[h, lanes, : s * strip], NT_DIMS,
                preferred_element_type=jnp.float32,
            )
        acc[h * count : (h + 1) * count, lanes] = value

    def off_chunk(h, d):
        @pl.when(c >= d)
        def _():
            off_copies[h, d].wait()
            at = jnp.maximum(c - d, 0)
            acc[h * count : (h + 1) * count, :] += lax.dot_general(
                zpeer[at, h], doff[h, d - 1], NT_DIMS, preferred_element_type=jnp.float32
            )

    work = [functools.partial(diag_chunk, h, s) for h in range(2) for s in range(strips)]
    spare = [functools.partial(off_chunk, h, d) for h in range(2) for d in range(1, cols)]

    def some(n):
        for _ in range(n):
            if work:
                work.pop(0)()

    some(strips)
    offsets = []
    for d in range(1, layers):
        offsets += [(d, a + d < layers, jnp.minimum(a + d, layers - 1) * PLANE + b, (0, 1))]
        offsets += [(-d, a - d >= 0, jnp.maximum(a - d, 0) * PLANE + b, (0,))]
    for d, there, owner, kinds in offsets:
        for h in kinds:
            j = tile_of(owner, h)
            z_wait(owner, h, there)
            z_push(zbuf.at[j], owner, h, row_down if d > 0 else row_up, there & (can_down if d > 0 else can_up))
            z_push(zbuf.at[j], owner, h, near[h], there)
            z_push(zbuf.at[j], owner, h, far[h], there)
        some(1)
    some(len(work))
    for i, peer in enumerate(col_peers):
        remote(z_ref, zpeer.at[peer], zp_send.at[i], zp_recv.at[peer], r, peer).wait_recv()
    second_step = (y_step, x_step)
    for d, there, owner, kinds in [(0, None, r, (0, 1))] + offsets:
        for h in kinds:
            from_near = owner + second_step[h]
            z_wait(from_near, h, there)
            j = tile_of(from_near, h)
            z_push(zbuf.at[j], from_near, h, far[h], there)
        if spare:
            spare.pop(0)()
    while spare:
        spare.pop(0)()
    last_step = (x_step, y_step)
    for d, there, owner, kinds in [(0, None, r, (0, 1))] + offsets:
        for h in kinds:
            z_wait(owner + last_step[h], h, there)
            z_wait(owner + x_step + y_step, h, there)

    group = 256 // rank
    lane_slot = lax.div(lax.broadcasted_iota(jnp.int32, (count, group * rank), 1), rank)
    lane_rank = lax.rem(lax.broadcasted_iota(jnp.int32, (count, group * rank), 1), rank)
    waited = 0
    for g in range(tiles // group):
        while waited * part < (g + 1) * group * rank:
            v_copies[waited].wait()
            waited += 1
        chosen = []
        for i in range(group):
            k = g * group + i
            chosen.append(zbuf[jnp.where(k < r, k, jnp.maximum(k - r, 0))].astype(jnp.float32))
        lhs = jnp.concatenate(chosen, axis=0).astype(jnp.bfloat16)
        span = pl.ds(g * group * rank, group * rank)
        result = lax.dot_general(lhs, vbuf[span, :], NT_DIMS, preferred_element_type=jnp.float32)
        value = result[:count]
        for i in range(1, group):
            value = jnp.where(lane_slot == i, result[i * count : (i + 1) * count], value)
        proj[c, :, span] = value
    for i, peer in enumerate(col_peers):
        push(proj.at[c], proj.at[c], pj_send.at[i], pj_recv.at[c], r, peer)
    for copy in u_copies:
        copy.wait()
    for i, peer in enumerate(col_peers):
        remote(proj.at[c], proj.at[peer], pj_send.at[i], pj_recv.at[peer], r, peer).wait_recv()
    weighted = []
    for g in range(tiles // group):
        span = pl.ds(g * group * rank, group * rank)
        value = proj[0, :, span]
        for k in range(1, cols):
            value = value + proj[k, :, span]
        limit = jnp.zeros((count, group * rank), jnp.int32)
        for i in range(group):
            limit = jnp.where(lane_slot == i, ranks_ref[0, g * group + i], limit)
        value = jnp.where(lane_rank < limit, value, 0.0)
        slot = lane_slot + g * group
        weighted.append(
            jnp.concatenate(
                [
                    jnp.where(slot < r, value, 0.0),
                    jnp.where((slot >= r) & (slot < tiles - 1), value, 0.0),
                ],
                axis=0,
            ).astype(jnp.bfloat16)
        )
    weights = jnp.concatenate(weighted, axis=1)
    value = acc[...] + jnp.dot(weights, ubuf[...], preferred_element_type=jnp.float32)
    full[c] = value
    sbf[...] = value.astype(jnp.bfloat16)
    for i, peer in enumerate(col_peers):
        push(full.at[c], full.at[c], sm_send.at[i], sm_recv.at[c], r, peer)
    prev_copies = [
        remote(sbf, prev.at[c], pv_send.at[k], pv_recv.at[c], jnp.minimum(r + 1, rows - 1), k)
        for k in range(cols)
    ]

    @pl.when(r < rows - 1)
    def _():
        for copy in prev_copies:
            copy.start()

    for h in range(2):
        samples_ref[h] = value[h * count : (h + 1) * count]
    for i, peer in enumerate(col_peers):
        remote(full.at[c], full.at[peer], sm_send.at[i], sm_recv.at[peer], r, peer).wait_recv()

    groups = first_ref.shape[0]
    per_row = shard // LANES
    own_first = 2 * tile // LANES
    batch = 4

    def table(ref, h, j):
        return ref[j // per_row, h * count : (h + 1) * count, (j % per_row) * LANES : (j % per_row + 1) * LANES]

    def split(ref, at):
        index = jnp.broadcast_to(ref[pl.ds(at, 1), :], (count, LANES))
        return lax.shift_right_logical(index, 7), lax.bitwise_and(index, LANES - 1)

    def pick(entry, low):
        return jnp.take_along_axis(entry, low, axis=1, mode="promise_in_bounds")

    def own_part(step, carry):
        ats = [step * batch + i for i in range(batch)]
        one = [split(first_ref, at) for at in ats]
        two = [split(second_ref, at) for at in ats]
        got_one = [jnp.zeros((count, LANES), jnp.float32) for _ in ats]
        got_two = [jnp.zeros((count, LANES), jnp.float32) for _ in ats]
        for got, index in ((got_one, one), (got_two, two)):
            for i in range(batch):
                for h in range(2):
                    for j in range(tile // LANES):
                        entry = table(full, h, j)
                        number = own_first + h * (tile // LANES) + j
                        got[i] = jnp.where(index[i][0] == number, pick(entry, index[i][1]), got[i])
        for i in range(batch):
            diff[ats[i]] = got_one[i] - got_two[i]
        return carry

    lax.fori_loop(0, groups // batch, own_part, 0)

    @pl.when(r > 0)
    def _():
        for k in range(cols):
            remote(sbf, prev.at[k], pv_send.at[k], pv_recv.at[k], r, c).wait_recv()
        prev32[...] = prev[...].astype(jnp.float32)

    @pl.when(r == 0)
    def _():
        prev32[...] = jnp.zeros_like(prev32)

    bin_rows = lax.broadcasted_iota(jnp.int32, (NBIN, LANES), 0)

    def prev_part(step, sums):
        ats = [step * batch + i for i in range(batch)]
        two = [split(second_ref, at) for at in ats]
        got = [jnp.zeros((count, LANES), jnp.float32) for _ in ats]
        for i in range(batch):
            for h in range(2):
                for j in range(tile // LANES):
                    entry = table(prev32, h, j)
                    number = h * (tile // LANES) + j
                    got[i] = jnp.where(two[i][0] == number, pick(entry, two[i][1]), got[i])
        for i in range(batch):
            differ = diff[ats[i]] - got[i]
            half_sq = 0.5 * differ * differ
            high = half_sq.astype(jnp.bfloat16).astype(jnp.float32)
            terms = jnp.concatenate(
                [high, half_sq - high, jnp.ones((count, LANES), jnp.float32)], axis=0
            ).astype(jnp.bfloat16)
            onehot = jnp.where(
                jnp.broadcast_to(bins_ref[pl.ds(ats[i], 1), :], (NBIN, LANES)) == bin_rows, 1.0, 0.0
            ).astype(jnp.bfloat16)
            sums = sums + lax.dot_general(terms, onehot, NT_DIMS, preferred_element_type=jnp.float32)
        return sums

    sums = lax.fori_loop(0, groups // batch, prev_part, jnp.zeros((3 * count, NBIN), jnp.float32))
    total = jnp.concatenate([sums[:count] + sums[count : 2 * count], sums[2 * count :]], axis=0)

    def reduce_stage(value, buf, at, peers, send, recv, number):
        buf[at] = value
        for i, (row, col, slot) in enumerate(peers):
            push(buf.at[at], buf.at[at], send.at[i], recv.at[at], row, col)
        for i, (row, col, slot) in enumerate(peers):
            remote(buf.at[at], buf.at[slot], send.at[i], recv.at[slot], row, col).wait_recv()
        out = buf[0]
        for i in range(1, number):
            out = out + buf[i]
        return out

    total = reduce_stage(total, red1, c, [(r, p, p) for p in col_peers], r1_send, r1_recv, cols)
    total = reduce_stage(
        total, red2, b, [(p, c, lax.rem(p, PLANE)) for p in plane_peers], r2_send, r2_recv, PLANE
    )
    total = reduce_stage(
        total, red3, a, [(p, c, lax.div(p, PLANE)) for p in layer_peers], r3_send, r3_recv, layers
    )
    vario_ref[...] = total[:count] / jnp.maximum(total[count:], 1.0)

    for copy in pending:
        copy.wait_send()
    for cond, copy in guarded:
        pl.when(cond)(copy.wait_send)

    @pl.when(r < rows - 1)
    def _():
        for copy in prev_copies:
            copy.wait_send()


def body(
    noise, diag_factor, left_factor, right_factor, tile_ranks, pair_first, pair_partner, bin_ids
):
    rows = lax.axis_size("row")
    cols = lax.axis_size("col")
    count = noise.shape[0]
    shard = noise.shape[3]
    tile = shard * cols
    tiles = 2 * rows
    rank = right_factor.shape[2]
    strip = min(256, shard)
    layers = rows // PLANE
    v_parts = 4
    z = jnp.transpose(noise[:, :, 0], (1, 0, 2))
    dma = lambda *shape: pltpu.SemaphoreType.DMA(shape)
    vmem = pl.BlockSpec(memory_space=pltpu.VMEM)
    hbm = pl.BlockSpec(memory_space=pl.ANY)
    smem = pl.BlockSpec(memory_space=pltpu.SMEM)
    off = max(cols - 1, 1)
    f32, bf16 = jnp.float32, jnp.bfloat16
    samples, vario = pl.pallas_call(
        functools.partial(kernel, (rows, cols, count, shard, tile, rank, strip)),
        out_shape=(
            jax.ShapeDtypeStruct((2, count, shard), f32),
            jax.ShapeDtypeStruct((count, NBIN), f32),
        ),
        in_specs=[vmem, hbm, hbm, hbm, smem, vmem, vmem, vmem],
        out_specs=(vmem, vmem),
        scratch_shapes=[
            pltpu.VMEM((tiles, count, shard), bf16),
            pltpu.VMEM((cols, 2, count, shard), bf16),
            pltpu.VMEM((2, shard, shard), bf16),
            pltpu.VMEM((2, off, shard, shard), bf16),
            pltpu.VMEM((tiles * rank, shard), bf16),
            pltpu.VMEM((tiles * rank, shard), bf16),
            pltpu.VMEM((cols, count, tiles * rank), f32),
            pltpu.VMEM((2 * count, shard), f32),
            pltpu.VMEM((cols, 2 * count, shard), f32),
            pltpu.VMEM((2 * count, shard), bf16),
            pltpu.VMEM((cols, 2 * count, shard), bf16),
            pltpu.VMEM((cols, 2 * count, shard), f32),
            pltpu.VMEM((pair_first.shape[2] // LANES, count, LANES), f32),
            pltpu.VMEM((cols, 2 * count, NBIN), f32),
            pltpu.VMEM((PLANE, 2 * count, NBIN), f32),
            pltpu.VMEM((layers, 2 * count, NBIN), f32),
            dma(2, shard // strip), dma(2, off), dma(v_parts), dma(v_parts),
            dma(16 * layers), dma(tiles), dma(off), dma(cols),
            dma(off), dma(cols), dma(off), dma(cols), dma(cols), dma(cols),
            dma(off), dma(cols), dma(PLANE), dma(PLANE), dma(layers), dma(layers),
        ],
        compiler_params=pltpu.CompilerParams(collective_id=0, has_side_effects=True),
    )(
        z,
        diag_factor.reshape(2, shard, tile),
        left_factor.reshape(tiles * rank, shard),
        right_factor.reshape(tiles * rank, shard),
        tile_ranks,
        pair_first.reshape(-1, LANES),
        pair_partner.reshape(-1, LANES),
        bin_ids.reshape(-1, LANES),
    )
    return jnp.transpose(samples, (1, 0, 2))[:, :, None, :], vario


def solution(mesh):
    in_specs = (
        P(None, None, "row", "col"),
        P(None, "row", "col", None),
        P("row", None, None, "col"),
        P("row", None, None, "col"),
        P("row", None),
        P("row", "col", None),
        P("row", "col", None),
        P("row", "col", None),
    )
    out_specs = (P(None, None, "row", "col"), P())
    return jax.shard_map(body, mesh=mesh, in_specs=in_specs, out_specs=out_specs, check_vma=False)
```

```python
import functools

import jax
import jax.numpy as jnp
from jax import lax
from jax.experimental import pallas as pl
from jax.experimental.pallas import tpu as pltpu
from jax.sharding import PartitionSpec as P

NBIN = 128
LANES = 128
PLANE = 4
MESH = pl.DeviceIdType.MESH
NT_DIMS = (((1,), (1,)), ((), ()))


def kernel(
    dims,
    noise_ref, diag_ref, left_ref, right_ref, ranks_ref, first_ref, second_ref, bins_ref,
    samples_ref, vario_ref,
    z_ref, zbuf, zpeer, down, doff, vbuf, ubuf, proj, acc, full, sbf, prev, prev32, diff, red1, red3,
    own_sem, off_sem, v_sem, u_sem,
    z_send, z_recv, zp_send, zp_recv, pj_send, pj_recv, sm_send, sm_recv, pv_send, pv_recv,
    r1_send, r1_recv, r3_send, r3_recv,
):
    rows, cols, count, shard, tile, rank, strip = dims
    layers = rows // PLANE
    tiles = 2 * rows
    r = lax.axis_index("row")
    c = lax.axis_index("col")
    b = lax.rem(r, PLANE)
    a = lax.div(r, PLANE)
    x_at = lax.rem(r, 2)
    y_at = lax.div(b, 2)
    x_step = 1 - 2 * x_at
    y_step = 2 - 4 * y_at
    strips = shard // strip
    pending = []

    def remote(src, dst, send, recv, row, col):
        return pltpu.make_async_remote_copy(
            src_ref=src, dst_ref=dst, send_sem=send, recv_sem=recv,
            device_id=(row, col), device_id_type=MESH,
        )

    def push(*args):
        copy = remote(*args)
        copy.start()
        pending.append(copy)

    own_copies = {}
    off_copies = {}
    for h in range(2):
        for s in range(strips):
            width = (s + 1) * strip
            own_copies[h, s] = pltpu.make_async_copy(
                diag_ref.at[h, pl.ds(s * strip, strip), pl.ds(pl.multiple_of(c * shard, LANES), width)],
                down.at[h, pl.ds(s * strip, strip), pl.ds(0, width)],
                own_sem.at[h, s],
            )
            own_copies[h, s].start()
    for h in range(2):
        for d in range(1, cols):
            at = jnp.maximum(c - d, 0)
            off_copies[h, d] = pltpu.make_async_copy(
                diag_ref.at[h, :, pl.ds(pl.multiple_of(at * shard, LANES), shard)],
                doff.at[h, d - 1],
                off_sem.at[h, d - 1],
            )

            @pl.when(c >= d)
            def _(copy=off_copies[h, d]):
                copy.start()

    v_parts = v_sem.shape[0]
    part = tiles * rank // v_parts
    v_copies = [
        pltpu.make_async_copy(right_ref.at[pl.ds(i * part, part)], vbuf.at[pl.ds(i * part, part)], v_sem.at[i])
        for i in range(v_parts)
    ]
    u_copies = [
        pltpu.make_async_copy(left_ref.at[pl.ds(i * part, part)], ubuf.at[pl.ds(i * part, part)], u_sem.at[i])
        for i in range(v_parts)
    ]
    for copy in v_copies + u_copies:
        copy.start()

    for h in range(2):
        z_ref[h] = noise_ref[...].astype(jnp.float32)[:, h].astype(jnp.bfloat16)

    barrier = pltpu.get_barrier_semaphore()

    def greet(row, col):
        pl.semaphore_signal(barrier, inc=1, device_id=(row, col), device_id_type=MESH)

    col_peers = [lax.rem(c + d, cols) for d in range(1, cols)]
    place = b * cols + c
    block_slots = [lax.rem(place + d, PLANE * cols) for d in range(1, PLANE * cols)]
    block_peers = [(a * PLANE + lax.div(m, cols), lax.rem(m, cols), m) for m in block_slots]
    layer_peers = [lax.rem(a + d, layers) * PLANE + b for d in range(1, layers)]
    for row, col, slot in block_peers:
        greet(row, col)

    @pl.when(a < layers - 1)
    def _():
        greet(r + PLANE, c)

    @pl.when(a > 0)
    def _():
        greet(r - PLANE, c)

    @pl.when(r < rows - 1)
    def _():
        for k in range(cols):
            greet(r + 1, k)

    @pl.when(r > 0)
    def _():
        for k in range(cols):
            greet(r - 1, k)

    expected = PLANE * cols - 1
    expected = expected + jnp.where(a < layers - 1, 1, 0) + jnp.where(a > 0, 1, 0)
    expected = expected + jnp.where(r < rows - 1, cols, 0) + jnp.where(r > 0, cols, 0)
    pl.semaphore_wait(barrier, expected)

    def tile_of(owner, h):
        return owner if h == 0 else tiles - 1 - owner

    send_at = [0]
    guarded = []

    def z_push(src, owner, h, row, cond=None):
        j = tile_of(owner, h)
        copy = remote(src, zbuf.at[j], z_send.at[send_at[0]], z_recv.at[j], row, c)
        send_at[0] += 1
        if cond is None:
            copy.start()
            pending.append(copy)
        else:
            guarded.append((cond, copy))
            pl.when(cond)(copy.start)

    def z_wait(owner, h, cond=None):
        j = tile_of(owner, h)
        copy = remote(zbuf.at[j], zbuf.at[j], z_send.at[0], z_recv.at[j], r, c)
        if cond is None:
            copy.wait_recv()
        else:
            pl.when(cond)(copy.wait_recv)

    row_x = r + x_step
    row_y = r + y_step
    near = (row_y, row_x)
    far = (row_x, row_y)
    row_up = jnp.minimum(r + PLANE, rows - PLANE + b)
    row_down = jnp.maximum(r - PLANE, b)
    can_up = a < layers - 1
    can_down = a > 0
    z_push(z_ref.at[0], r, 0, row_down, can_down)
    z_push(z_ref.at[0], r, 0, row_up, can_up)
    z_push(z_ref.at[1], r, 1, row_down, can_down)
    for h in range(2):
        z_push(z_ref.at[h], r, h, near[h])
        z_push(z_ref.at[h], r, h, far[h])
    for i, peer in enumerate(col_peers):
        push(z_ref, zpeer.at[c], zp_send.at[i], zp_recv.at[c], r, peer)
    for h in range(2):
        zbuf[tile_of(r, h)] = z_ref[h]

    def diag_chunk(h, s):
        own_copies[h, s].wait()
        lanes = pl.ds(s * strip, strip)
        block = down[h, lanes, lanes]
        below = (
            lax.broadcasted_iota(jnp.int32, (strip, strip), 1)
            < lax.broadcasted_iota(jnp.int32, (strip, strip), 0)
        )
        block = jnp.where(below, block.astype(jnp.float32), 0.0).astype(jnp.bfloat16)
        mine = z_ref[h, :, lanes]
        value = mine.astype(jnp.float32)
        value += lax.dot_general(mine, block, NT_DIMS, preferred_element_type=jnp.float32)
        if s:
            value += lax.dot_general(
                z_ref[h, :, : s * strip], down[h, lanes, : s * strip], NT_DIMS,
                preferred_element_type=jnp.float32,
            )
        acc[h * count : (h + 1) * count, lanes] = value

    def off_chunk(h, d):
        @pl.when(c >= d)
        def _():
            off_copies[h, d].wait()
            at = jnp.maximum(c - d, 0)
            acc[h * count : (h + 1) * count, :] += lax.dot_general(
                zpeer[at, h], doff[h, d - 1], NT_DIMS, preferred_element_type=jnp.float32
            )

    work = [functools.partial(diag_chunk, h, s) for h in range(2) for s in range(strips)]
    spare = [functools.partial(off_chunk, h, d) for h in range(2) for d in range(1, cols)]

    def some(n):
        for _ in range(n):
            if work:
                work.pop(0)()

    some(strips)
    offsets = []
    for d in range(1, layers):
        offsets += [(d, a + d < layers, jnp.minimum(a + d, layers - 1) * PLANE + b, (0, 1))]
        offsets += [(-d, a - d >= 0, jnp.maximum(a - d, 0) * PLANE + b, (0,))]
    for d, there, owner, kinds in offsets:
        for h in kinds:
            j = tile_of(owner, h)
            z_wait(owner, h, there)
            z_push(zbuf.at[j], owner, h, row_down if d > 0 else row_up, there & (can_down if d > 0 else can_up))
            z_push(zbuf.at[j], owner, h, near[h], there)
            z_push(zbuf.at[j], owner, h, far[h], there)
        some(1)
    some(len(work))
    for i, peer in enumerate(col_peers):
        remote(z_ref, zpeer.at[peer], zp_send.at[i], zp_recv.at[peer], r, peer).wait_recv()
    second_step = (y_step, x_step)
    for d, there, owner, kinds in [(0, None, r, (0, 1))] + offsets:
        for h in kinds:
            from_near = owner + second_step[h]
            z_wait(from_near, h, there)
            j = tile_of(from_near, h)
            z_push(zbuf.at[j], from_near, h, far[h], there)
        if spare:
            spare.pop(0)()
    while spare:
        spare.pop(0)()
    last_step = (x_step, y_step)
    for d, there, owner, kinds in [(0, None, r, (0, 1))] + offsets:
        for h in kinds:
            z_wait(owner + last_step[h], h, there)
            z_wait(owner + x_step + y_step, h, there)

    group = 256 // rank
    lane_slot = lax.div(lax.broadcasted_iota(jnp.int32, (count, group * rank), 1), rank)
    lane_rank = lax.rem(lax.broadcasted_iota(jnp.int32, (count, group * rank), 1), rank)
    waited = 0
    for g in range(tiles // group):
        while waited * part < (g + 1) * group * rank:
            v_copies[waited].wait()
            waited += 1
        chosen = []
        for i in range(group):
            k = g * group + i
            chosen.append(zbuf[jnp.where(k < r, k, jnp.maximum(k - r, 0))].astype(jnp.float32))
        lhs = jnp.concatenate(chosen, axis=0).astype(jnp.bfloat16)
        span = pl.ds(g * group * rank, group * rank)
        result = lax.dot_general(lhs, vbuf[span, :], NT_DIMS, preferred_element_type=jnp.float32)
        value = result[:count]
        for i in range(1, group):
            value = jnp.where(lane_slot == i, result[i * count : (i + 1) * count], value)
        proj[c, :, span] = value
    for i, peer in enumerate(col_peers):
        push(proj.at[c], proj.at[c], pj_send.at[i], pj_recv.at[c], r, peer)
    for copy in u_copies:
        copy.wait()
    for i, peer in enumerate(col_peers):
        remote(proj.at[c], proj.at[peer], pj_send.at[i], pj_recv.at[peer], r, peer).wait_recv()
    weighted = []
    for g in range(tiles // group):
        span = pl.ds(g * group * rank, group * rank)
        value = proj[0, :, span]
        for k in range(1, cols):
            value = value + proj[k, :, span]
        limit = jnp.zeros((count, group * rank), jnp.int32)
        for i in range(group):
            limit = jnp.where(lane_slot == i, ranks_ref[0, g * group + i], limit)
        value = jnp.where(lane_rank < limit, value, 0.0)
        slot = lane_slot + g * group
        weighted.append(
            jnp.concatenate(
                [
                    jnp.where(slot < r, value, 0.0),
                    jnp.where((slot >= r) & (slot < tiles - 1), value, 0.0),
                ],
                axis=0,
            ).astype(jnp.bfloat16)
        )
    weights = jnp.concatenate(weighted, axis=1)
    value = acc[...] + jnp.dot(weights, ubuf[...], preferred_element_type=jnp.float32)
    full[c] = value
    sbf[...] = value.astype(jnp.bfloat16)
    for i, peer in enumerate(col_peers):
        push(full.at[c], full.at[c], sm_send.at[i], sm_recv.at[c], r, peer)
    prev_copies = [
        remote(sbf, prev.at[c], pv_send.at[k], pv_recv.at[c], jnp.minimum(r + 1, rows - 1), k)
        for k in range(cols)
    ]

    @pl.when(r < rows - 1)
    def _():
        for copy in prev_copies:
            copy.start()

    for h in range(2):
        samples_ref[:, h, 0, :] = value[h * count : (h + 1) * count]
    groups = first_ref.shape[0]
    per_row = shard // LANES
    own_first = 2 * tile // LANES
    batch = 4

    def table(ref, h, j):
        return ref[j // per_row, h * count : (h + 1) * count, (j % per_row) * LANES : (j % per_row + 1) * LANES]

    def split(ref, at):
        index = jnp.broadcast_to(ref[pl.ds(at, 1), :], (count, LANES))
        return lax.shift_right_logical(index, 7), lax.bitwise_and(index, LANES - 1)

    def pick(entry, low):
        return jnp.take_along_axis(entry, low, axis=1, mode="promise_in_bounds")

    def own_part(k, fresh, step, carry):
        ats = [step * batch + i for i in range(batch)]
        base = own_first + k * per_row
        got = [[], []]
        for which, ref in enumerate((first_ref, second_ref)):
            for at in ats:
                high, low = split(ref, at)
                high = high - base
                value = jnp.zeros((count, LANES), jnp.float32)
                for h in range(2):
                    for j in range(per_row):
                        entry = full[k, h * count : (h + 1) * count, j * LANES : (j + 1) * LANES]
                        value = jnp.where(high == h * (tile // LANES) + j, pick(entry, low), value)
                got[which].append(value)
        for i in range(batch):
            value = got[0][i] - got[1][i]
            diff[ats[i]] = value if fresh else diff[ats[i]] + value
        return carry

    lax.fori_loop(0, groups // batch, functools.partial(own_part, c, True), 0)
    for i, peer in enumerate(col_peers):
        remote(full.at[c], full.at[peer], sm_send.at[i], sm_recv.at[peer], r, peer).wait_recv()
        lax.fori_loop(0, groups // batch, functools.partial(own_part, peer, False), 0)

    @pl.when(r > 0)
    def _():
        for k in range(cols):
            remote(sbf, prev.at[k], pv_send.at[k], pv_recv.at[k], r, c).wait_recv()
        prev32[...] = prev[...].astype(jnp.float32)

    @pl.when(r == 0)
    def _():
        prev32[...] = jnp.zeros_like(prev32)

    bin_rows = lax.broadcasted_iota(jnp.int32, (NBIN, LANES), 0)

    def prev_part(step, sums):
        ats = [step * batch + i for i in range(batch)]
        two = [split(second_ref, at) for at in ats]
        got = [jnp.zeros((count, LANES), jnp.float32) for _ in ats]
        for i in range(batch):
            for h in range(2):
                for j in range(tile // LANES):
                    entry = table(prev32, h, j)
                    number = h * (tile // LANES) + j
                    got[i] = jnp.where(two[i][0] == number, pick(entry, two[i][1]), got[i])
        for i in range(batch):
            differ = diff[ats[i]] - got[i]
            half_sq = 0.5 * differ * differ
            high = half_sq.astype(jnp.bfloat16).astype(jnp.float32)
            terms = jnp.concatenate(
                [high, half_sq - high, jnp.ones((count, LANES), jnp.float32)], axis=0
            ).astype(jnp.bfloat16)
            onehot = jnp.where(
                jnp.broadcast_to(bins_ref[pl.ds(ats[i], 1), :], (NBIN, LANES)) == bin_rows, 1.0, 0.0
            ).astype(jnp.bfloat16)
            sums = sums + lax.dot_general(terms, onehot, NT_DIMS, preferred_element_type=jnp.float32)
        return sums

    sums = lax.fori_loop(0, groups // batch, prev_part, jnp.zeros((3 * count, NBIN), jnp.float32))
    total = jnp.concatenate([sums[:count] + sums[count : 2 * count], sums[2 * count :]], axis=0)

    def reduce_stage(value, buf, at, peers, send, recv, number):
        buf[at] = value
        for i, (row, col, slot) in enumerate(peers):
            push(buf.at[at], buf.at[at], send.at[i], recv.at[at], row, col)
        for i, (row, col, slot) in enumerate(peers):
            remote(buf.at[at], buf.at[slot], send.at[i], recv.at[slot], row, col).wait_recv()
        out = buf[0]
        for i in range(1, number):
            out = out + buf[i]
        return out

    total = reduce_stage(total, red1, place, block_peers, r1_send, r1_recv, PLANE * cols)
    total = reduce_stage(
        total, red3, a, [(p, c, lax.div(p, PLANE)) for p in layer_peers], r3_send, r3_recv, layers
    )
    vario_ref[...] = total[:count] / jnp.maximum(total[count:], 1.0)

    for copy in pending:
        copy.wait_send()
    for cond, copy in guarded:
        pl.when(cond)(copy.wait_send)

    @pl.when(r < rows - 1)
    def _():
        for copy in prev_copies:
            copy.wait_send()


def body(
    noise, diag_factor, left_factor, right_factor, tile_ranks, pair_first, pair_partner, bin_ids
):
    rows = lax.axis_size("row")
    cols = lax.axis_size("col")
    count = noise.shape[0]
    shard = noise.shape[3]
    tile = shard * cols
    tiles = 2 * rows
    rank = right_factor.shape[2]
    strip = min(256, shard)
    layers = rows // PLANE
    v_parts = 4
    dma = lambda *shape: pltpu.SemaphoreType.DMA(shape)
    vmem = pl.BlockSpec(memory_space=pltpu.VMEM)
    hbm = pl.BlockSpec(memory_space=pl.ANY)
    smem = pl.BlockSpec(memory_space=pltpu.SMEM)
    off = max(cols - 1, 1)
    f32, bf16 = jnp.float32, jnp.bfloat16
    samples, vario = pl.pallas_call(
        functools.partial(kernel, (rows, cols, count, shard, tile, rank, strip)),
        out_shape=(
            jax.ShapeDtypeStruct((count, 2, 1, shard), f32),
            jax.ShapeDtypeStruct((count, NBIN), f32),
        ),
        in_specs=[vmem, hbm, hbm, hbm, smem, vmem, vmem, vmem],
        out_specs=(vmem, vmem),
        scratch_shapes=[
            pltpu.VMEM((2, count, shard), bf16),
            pltpu.VMEM((tiles, count, shard), bf16),
            pltpu.VMEM((cols, 2, count, shard), bf16),
            pltpu.VMEM((2, shard, shard), bf16),
            pltpu.VMEM((2, off, shard, shard), bf16),
            pltpu.VMEM((tiles * rank, shard), bf16),
            pltpu.VMEM((tiles * rank, shard), bf16),
            pltpu.VMEM((cols, count, tiles * rank), f32),
            pltpu.VMEM((2 * count, shard), f32),
            pltpu.VMEM((cols, 2 * count, shard), f32),
            pltpu.VMEM((2 * count, shard), bf16),
            pltpu.VMEM((cols, 2 * count, shard), bf16),
            pltpu.VMEM((cols, 2 * count, shard), f32),
            pltpu.VMEM((pair_first.shape[2] // LANES, count, LANES), f32),
            pltpu.VMEM((PLANE * cols, 2 * count, NBIN), f32),
            pltpu.VMEM((layers, 2 * count, NBIN), f32),
            dma(2, shard // strip), dma(2, off), dma(v_parts), dma(v_parts),
            dma(16 * layers), dma(tiles), dma(off), dma(cols),
            dma(off), dma(cols), dma(off), dma(cols), dma(cols), dma(cols),
            dma(PLANE * cols), dma(PLANE * cols), dma(layers), dma(layers),
        ],
        compiler_params=pltpu.CompilerParams(collective_id=0, has_side_effects=True),
    )(
        noise.reshape(count, 2, shard),
        diag_factor.reshape(2, shard, tile),
        left_factor.reshape(tiles * rank, shard),
        right_factor.reshape(tiles * rank, shard),
        tile_ranks,
        pair_first.reshape(-1, LANES),
        pair_partner.reshape(-1, LANES),
        bin_ids.reshape(-1, LANES),
    )
    return samples, vario


def solution(mesh):
    in_specs = (
        P(None, None, "row", "col"),
        P(None, "row", "col", None),
        P("row", None, None, "col"),
        P("row", None, None, "col"),
        P("row", None),
        P("row", "col", None),
        P("row", "col", None),
        P("row", "col", None),
    )
    out_specs = (P(None, None, "row", "col"), P())
    return jax.shard_map(body, mesh=mesh, in_specs=in_specs, out_specs=out_specs, check_vma=False)
```

```python
import functools

import jax
import jax.numpy as jnp
from jax import lax
from jax.experimental import pallas as pl
from jax.experimental.pallas import tpu as pltpu
from jax.sharding import PartitionSpec as P

NBIN = 128
LANES = 128
PLANE = 4
MESH = pl.DeviceIdType.MESH
NT_DIMS = (((1,), (1,)), ((), ()))


def kernel(
    dims,
    noise_ref, diag_ref, left_ref, right_ref, ranks_ref, first_ref, second_ref, bins_ref,
    samples_ref, vario_ref,
    z_ref, zbuf, zpeer, down, doff, vbuf, ubuf, proj, acc, full, sbf, prev, prev32, diff, red1, red3,
    own_sem, off_sem, v_sem, u_sem,
    z_send, z_recv, zp_send, zp_recv, pj_send, pj_recv, sm_send, sm_recv, pv_send, pv_recv,
    r1_send, r1_recv, r3_send, r3_recv,
):
    rows, cols, count, shard, tile, rank, strip = dims
    layers = rows // PLANE
    tiles = 2 * rows
    r = lax.axis_index("row")
    c = lax.axis_index("col")
    b = lax.rem(r, PLANE)
    a = lax.div(r, PLANE)
    x_at = lax.rem(r, 2)
    y_at = lax.div(b, 2)
    x_step = 1 - 2 * x_at
    y_step = 2 - 4 * y_at
    strips = shard // strip
    pending = []

    def remote(src, dst, send, recv, row, col):
        return pltpu.make_async_remote_copy(
            src_ref=src, dst_ref=dst, send_sem=send, recv_sem=recv,
            device_id=(row, col), device_id_type=MESH,
        )

    def push(*args):
        copy = remote(*args)
        copy.start()
        pending.append(copy)

    own_copies = {}
    off_copies = {}
    for h in range(2):
        for s in range(strips):
            width = (s + 1) * strip
            own_copies[h, s] = pltpu.make_async_copy(
                diag_ref.at[h, pl.ds(s * strip, strip), pl.ds(pl.multiple_of(c * shard, LANES), width)],
                down.at[h, pl.ds(s * strip, strip), pl.ds(0, width)],
                own_sem.at[h, s],
            )
            own_copies[h, s].start()
    for h in range(2):
        for d in range(1, cols):
            at = jnp.maximum(c - d, 0)
            off_copies[h, d] = pltpu.make_async_copy(
                diag_ref.at[h, :, pl.ds(pl.multiple_of(at * shard, LANES), shard)],
                doff.at[h, d - 1],
                off_sem.at[h, d - 1],
            )

            @pl.when(c >= d)
            def _(copy=off_copies[h, d]):
                copy.start()

    v_parts = v_sem.shape[0]
    part = tiles * rank // v_parts
    v_copies = [
        pltpu.make_async_copy(right_ref.at[pl.ds(i * part, part)], vbuf.at[pl.ds(i * part, part)], v_sem.at[i])
        for i in range(v_parts)
    ]
    u_copies = [
        pltpu.make_async_copy(left_ref.at[pl.ds(i * part, part)], ubuf.at[pl.ds(i * part, part)], u_sem.at[i])
        for i in range(v_parts)
    ]
    for copy in v_copies + u_copies:
        copy.start()

    for h in range(2):
        z_ref[h] = noise_ref[...].astype(jnp.float32)[:, h].astype(jnp.bfloat16)

    barrier = pltpu.get_barrier_semaphore()

    def greet(row, col):
        pl.semaphore_signal(barrier, inc=1, device_id=(row, col), device_id_type=MESH)

    col_peers = [lax.rem(c + d, cols) for d in range(1, cols)]
    place = b * cols + c
    block_slots = [lax.rem(place + d, PLANE * cols) for d in range(1, PLANE * cols)]
    block_peers = [(a * PLANE + lax.div(m, cols), lax.rem(m, cols), m) for m in block_slots]
    layer_peers = [lax.rem(a + d, layers) * PLANE + b for d in range(1, layers)]
    for row, col, slot in block_peers:
        greet(row, col)

    for peer in layer_peers:
        greet(peer, c)

    @pl.when(r < rows - 1)
    def _():
        for k in range(cols):
            greet(r + 1, k)

    @pl.when(r > 0)
    def _():
        for k in range(cols):
            greet(r - 1, k)

    expected = PLANE * cols - 1 + layers - 1
    expected = expected + jnp.where(r < rows - 1, cols, 0) + jnp.where(r > 0, cols, 0)
    pl.semaphore_wait(barrier, expected)

    def tile_of(owner, h):
        return owner if h == 0 else tiles - 1 - owner

    send_at = [0]
    guarded = []

    def z_push(src, owner, h, row, cond=None):
        j = tile_of(owner, h)
        copy = remote(src, zbuf.at[j], z_send.at[send_at[0]], z_recv.at[j], row, c)
        send_at[0] += 1
        if cond is None:
            copy.start()
            pending.append(copy)
        else:
            guarded.append((cond, copy))
            pl.when(cond)(copy.start)

    def z_wait(owner, h, cond=None):
        j = tile_of(owner, h)
        copy = remote(zbuf.at[j], zbuf.at[j], z_send.at[0], z_recv.at[j], r, c)
        if cond is None:
            copy.wait_recv()
        else:
            pl.when(cond)(copy.wait_recv)

    row_x = r + x_step
    row_y = r + y_step
    near = (row_y, row_x)
    far = (row_x, row_y)
    others = []
    for d in range(1, layers):
        other = lax.rem(a + jnp.where(2 * a < layers, d, layers - d), layers)
        others.append((other, other * PLANE + b))
    for other, peer in others:
        z_push(z_ref.at[0], r, 0, peer)
        z_push(z_ref.at[1], r, 1, peer, other < a)
    for h in range(2):
        z_push(z_ref.at[h], r, h, near[h])
        z_push(z_ref.at[h], r, h, far[h])
    for i, peer in enumerate(col_peers):
        push(z_ref, zpeer.at[c], zp_send.at[i], zp_recv.at[c], r, peer)
    for h in range(2):
        zbuf[tile_of(r, h)] = z_ref[h]

    def diag_chunk(h, s):
        own_copies[h, s].wait()
        lanes = pl.ds(s * strip, strip)
        block = down[h, lanes, lanes]
        below = (
            lax.broadcasted_iota(jnp.int32, (strip, strip), 1)
            < lax.broadcasted_iota(jnp.int32, (strip, strip), 0)
        )
        block = jnp.where(below, block.astype(jnp.float32), 0.0).astype(jnp.bfloat16)
        mine = z_ref[h, :, lanes]
        value = mine.astype(jnp.float32)
        value += lax.dot_general(mine, block, NT_DIMS, preferred_element_type=jnp.float32)
        if s:
            value += lax.dot_general(
                z_ref[h, :, : s * strip], down[h, lanes, : s * strip], NT_DIMS,
                preferred_element_type=jnp.float32,
            )
        acc[h * count : (h + 1) * count, lanes] = value

    def off_chunk(h, d):
        @pl.when(c >= d)
        def _():
            off_copies[h, d].wait()
            at = jnp.maximum(c - d, 0)
            acc[h * count : (h + 1) * count, :] += lax.dot_general(
                zpeer[at, h], doff[h, d - 1], NT_DIMS, preferred_element_type=jnp.float32
            )

    work = [functools.partial(diag_chunk, h, s) for h in range(2) for s in range(strips)]
    spare = [functools.partial(off_chunk, h, d) for h in range(2) for d in range(1, cols)]

    def some(n):
        for _ in range(n):
            if work:
                work.pop(0)()

    some(2)
    offsets = [(owner, (None, other > a)) for other, owner in others]
    for owner, there in offsets:
        for h in range(2):
            j = tile_of(owner, h)
            z_wait(owner, h, there[h])
            z_push(zbuf.at[j], owner, h, near[h], there[h])
            z_push(zbuf.at[j], owner, h, far[h], there[h])
        some(1)
    some(len(work))
    for i, peer in enumerate(col_peers):
        remote(z_ref, zpeer.at[peer], zp_send.at[i], zp_recv.at[peer], r, peer).wait_recv()
    second_step = (y_step, x_step)
    for owner, there in [(r, (None, None))] + offsets:
        for h in range(2):
            from_near = owner + second_step[h]
            z_wait(from_near, h, there[h])
            j = tile_of(from_near, h)
            z_push(zbuf.at[j], from_near, h, far[h], there[h])
        if spare:
            spare.pop(0)()
    while spare:
        spare.pop(0)()
    last_step = (x_step, y_step)
    for owner, there in [(r, (None, None))] + offsets:
        for h in range(2):
            z_wait(owner + last_step[h], h, there[h])
            z_wait(owner + x_step + y_step, h, there[h])

    group = 256 // rank
    lane_slot = lax.div(lax.broadcasted_iota(jnp.int32, (count, group * rank), 1), rank)
    lane_rank = lax.rem(lax.broadcasted_iota(jnp.int32, (count, group * rank), 1), rank)
    waited = 0
    for g in range(tiles // group):
        while waited * part < (g + 1) * group * rank:
            v_copies[waited].wait()
            waited += 1
        chosen = []
        for i in range(group):
            k = g * group + i
            chosen.append(zbuf[jnp.where(k < r, k, jnp.maximum(k - r, 0))].astype(jnp.float32))
        lhs = jnp.concatenate(chosen, axis=0).astype(jnp.bfloat16)
        span = pl.ds(g * group * rank, group * rank)
        result = lax.dot_general(lhs, vbuf[span, :], NT_DIMS, preferred_element_type=jnp.float32)
        value = result[:count]
        for i in range(1, group):
            value = jnp.where(lane_slot == i, result[i * count : (i + 1) * count], value)
        proj[c, :, span] = value
    for i, peer in enumerate(col_peers):
        push(proj.at[c], proj.at[c], pj_send.at[i], pj_recv.at[c], r, peer)
    for copy in u_copies:
        copy.wait()
    for i, peer in enumerate(col_peers):
        remote(proj.at[c], proj.at[peer], pj_send.at[i], pj_recv.at[peer], r, peer).wait_recv()
    weighted = []
    for g in range(tiles // group):
        span = pl.ds(g * group * rank, group * rank)
        value = proj[0, :, span]
        for k in range(1, cols):
            value = value + proj[k, :, span]
        limit = jnp.zeros((count, group * rank), jnp.int32)
        for i in range(group):
            limit = jnp.where(lane_slot == i, ranks_ref[0, g * group + i], limit)
        value = jnp.where(lane_rank < limit, value, 0.0)
        slot = lane_slot + g * group
        weighted.append(
            jnp.concatenate(
                [
                    jnp.where(slot < r, value, 0.0),
                    jnp.where((slot >= r) & (slot < tiles - 1), value, 0.0),
                ],
                axis=0,
            ).astype(jnp.bfloat16)
        )
    weights = jnp.concatenate(weighted, axis=1)
    value = acc[...] + jnp.dot(weights, ubuf[...], preferred_element_type=jnp.float32)
    full[c] = value
    sbf[...] = value.astype(jnp.bfloat16)
    for i, peer in enumerate(col_peers):
        push(full.at[c], full.at[c], sm_send.at[i], sm_recv.at[c], r, peer)
    prev_copies = [
        remote(sbf, prev.at[c], pv_send.at[k], pv_recv.at[c], jnp.minimum(r + 1, rows - 1), k)
        for k in range(cols)
    ]

    @pl.when(r < rows - 1)
    def _():
        for copy in prev_copies:
            copy.start()

    for h in range(2):
        samples_ref[:, h, 0, :] = value[h * count : (h + 1) * count]
    groups = first_ref.shape[0]
    per_row = shard // LANES
    own_first = 2 * tile // LANES
    batch = 4

    def table(ref, h, j):
        return ref[j // per_row, h * count : (h + 1) * count, (j % per_row) * LANES : (j % per_row + 1) * LANES]

    def split(ref, at):
        index = jnp.broadcast_to(ref[pl.ds(at, 1), :], (count, LANES))
        return lax.shift_right_logical(index, 7), lax.bitwise_and(index, LANES - 1)

    def pick(entry, low):
        return jnp.take_along_axis(entry, low, axis=1, mode="promise_in_bounds")

    def own_part(k, fresh, step, carry):
        ats = [step * batch + i for i in range(batch)]
        base = own_first + k * per_row
        got = [[], []]
        for which, ref in enumerate((first_ref, second_ref)):
            for at in ats:
                high, low = split(ref, at)
                high = high - base
                value = jnp.zeros((count, LANES), jnp.float32)
                for h in range(2):
                    for j in range(per_row):
                        entry = full[k, h * count : (h + 1) * count, j * LANES : (j + 1) * LANES]
                        value = jnp.where(high == h * (tile // LANES) + j, pick(entry, low), value)
                got[which].append(value)
        for i in range(batch):
            value = got[0][i] - got[1][i]
            diff[ats[i]] = value if fresh else diff[ats[i]] + value
        return carry

    lax.fori_loop(0, groups // batch, functools.partial(own_part, c, True), 0)
    for i, peer in enumerate(col_peers):
        remote(full.at[c], full.at[peer], sm_send.at[i], sm_recv.at[peer], r, peer).wait_recv()
        lax.fori_loop(0, groups // batch, functools.partial(own_part, peer, False), 0)

    @pl.when(r > 0)
    def _():
        for k in range(cols):
            remote(sbf, prev.at[k], pv_send.at[k], pv_recv.at[k], r, c).wait_recv()
        prev32[...] = prev[...].astype(jnp.float32)

    @pl.when(r == 0)
    def _():
        prev32[...] = jnp.zeros_like(prev32)

    bin_rows = lax.broadcasted_iota(jnp.int32, (NBIN, LANES), 0)

    def prev_part(step, sums):
        ats = [step * batch + i for i in range(batch)]
        two = [split(second_ref, at) for at in ats]
        got = [jnp.zeros((count, LANES), jnp.float32) for _ in ats]
        for i in range(batch):
            for h in range(2):
                for j in range(tile // LANES):
                    entry = table(prev32, h, j)
                    number = h * (tile // LANES) + j
                    got[i] = jnp.where(two[i][0] == number, pick(entry, two[i][1]), got[i])
        for i in range(batch):
            differ = diff[ats[i]] - got[i]
            half_sq = 0.5 * differ * differ
            high = half_sq.astype(jnp.bfloat16).astype(jnp.float32)
            terms = jnp.concatenate(
                [high, half_sq - high, jnp.ones((count, LANES), jnp.float32)], axis=0
            ).astype(jnp.bfloat16)
            onehot = jnp.where(
                jnp.broadcast_to(bins_ref[pl.ds(ats[i], 1), :], (NBIN, LANES)) == bin_rows, 1.0, 0.0
            ).astype(jnp.bfloat16)
            sums = sums + lax.dot_general(terms, onehot, NT_DIMS, preferred_element_type=jnp.float32)
        return sums

    sums = lax.fori_loop(0, groups // batch, prev_part, jnp.zeros((3 * count, NBIN), jnp.float32))
    total = jnp.concatenate([sums[:count] + sums[count : 2 * count], sums[2 * count :]], axis=0)

    def reduce_stage(value, buf, at, peers, send, recv, number):
        buf[at] = value
        for i, (row, col, slot) in enumerate(peers):
            push(buf.at[at], buf.at[at], send.at[i], recv.at[at], row, col)
        for i, (row, col, slot) in enumerate(peers):
            remote(buf.at[at], buf.at[slot], send.at[i], recv.at[slot], row, col).wait_recv()
        out = buf[0]
        for i in range(1, number):
            out = out + buf[i]
        return out

    total = reduce_stage(total, red1, place, block_peers, r1_send, r1_recv, PLANE * cols)
    total = reduce_stage(
        total, red3, a, [(p, c, lax.div(p, PLANE)) for p in layer_peers], r3_send, r3_recv, layers
    )
    vario_ref[...] = total[:count] / jnp.maximum(total[count:], 1.0)

    for copy in pending:
        copy.wait_send()
    for cond, copy in guarded:
        pl.when(cond)(copy.wait_send)

    @pl.when(r < rows - 1)
    def _():
        for copy in prev_copies:
            copy.wait_send()


def body(
    noise, diag_factor, left_factor, right_factor, tile_ranks, pair_first, pair_partner, bin_ids
):
    rows = lax.axis_size("row")
    cols = lax.axis_size("col")
    count = noise.shape[0]
    shard = noise.shape[3]
    tile = shard * cols
    tiles = 2 * rows
    rank = right_factor.shape[2]
    strip = min(256, shard)
    layers = rows // PLANE
    v_parts = 4
    dma = lambda *shape: pltpu.SemaphoreType.DMA(shape)
    vmem = pl.BlockSpec(memory_space=pltpu.VMEM)
    hbm = pl.BlockSpec(memory_space=pl.ANY)
    smem = pl.BlockSpec(memory_space=pltpu.SMEM)
    off = max(cols - 1, 1)
    f32, bf16 = jnp.float32, jnp.bfloat16
    samples, vario = pl.pallas_call(
        functools.partial(kernel, (rows, cols, count, shard, tile, rank, strip)),
        out_shape=(
            jax.ShapeDtypeStruct((count, 2, 1, shard), f32),
            jax.ShapeDtypeStruct((count, NBIN), f32),
        ),
        in_specs=[vmem, hbm, hbm, hbm, smem, vmem, vmem, vmem],
        out_specs=(vmem, vmem),
        scratch_shapes=[
            pltpu.VMEM((2, count, shard), bf16),
            pltpu.VMEM((tiles, count, shard), bf16),
            pltpu.VMEM((cols, 2, count, shard), bf16),
            pltpu.VMEM((2, shard, shard), bf16),
            pltpu.VMEM((2, off, shard, shard), bf16),
            pltpu.VMEM((tiles * rank, shard), bf16),
            pltpu.VMEM((tiles * rank, shard), bf16),
            pltpu.VMEM((cols, count, tiles * rank), f32),
            pltpu.VMEM((2 * count, shard), f32),
            pltpu.VMEM((cols, 2 * count, shard), f32),
            pltpu.VMEM((2 * count, shard), bf16),
            pltpu.VMEM((cols, 2 * count, shard), bf16),
            pltpu.VMEM((cols, 2 * count, shard), f32),
            pltpu.VMEM((pair_first.shape[2] // LANES, count, LANES), f32),
            pltpu.VMEM((PLANE * cols, 2 * count, NBIN), f32),
            pltpu.VMEM((layers, 2 * count, NBIN), f32),
            dma(2, shard // strip), dma(2, off), dma(v_parts), dma(v_parts),
            dma(16 * layers), dma(tiles), dma(off), dma(cols),
            dma(off), dma(cols), dma(off), dma(cols), dma(cols), dma(cols),
            dma(PLANE * cols), dma(PLANE * cols), dma(layers), dma(layers),
        ],
        compiler_params=pltpu.CompilerParams(collective_id=0, has_side_effects=True),
    )(
        noise.reshape(count, 2, shard),
        diag_factor.reshape(2, shard, tile),
        left_factor.reshape(tiles * rank, shard),
        right_factor.reshape(tiles * rank, shard),
        tile_ranks,
        pair_first.reshape(-1, LANES),
        pair_partner.reshape(-1, LANES),
        bin_ids.reshape(-1, LANES),
    )
    return samples, vario


def solution(mesh):
    in_specs = (
        P(None, None, "row", "col"),
        P(None, "row", "col", None),
        P("row", None, None, "col"),
        P("row", None, None, "col"),
        P("row", None),
        P("row", "col", None),
        P("row", "col", None),
        P("row", "col", None),
    )
    out_specs = (P(None, None, "row", "col"), P())
    return jax.shard_map(body, mesh=mesh, in_specs=in_specs, out_specs=out_specs, check_vma=False)
```

```python
import functools

import jax
import jax.numpy as jnp
from jax import lax
from jax.experimental import pallas as pl
from jax.experimental.pallas import tpu as pltpu
from jax.sharding import PartitionSpec as P

NBIN = 128
LANES = 128
PLANE = 4
MESH = pl.DeviceIdType.MESH
NT_DIMS = (((1,), (1,)), ((), ()))


def kernel(
    dims,
    noise_ref, diag_ref, left_ref, right_ref, ranks_ref, first_ref, second_ref, bins_ref,
    samples_ref, vario_ref,
    z_ref, zbuf, zpeer, down, doff, vbuf, ubuf, proj, acc, full, sbf, prev, prev32, diff, red1, red3,
    own_sem, off_sem, v_sem, u_sem,
    z_send, z_recv, zp_send, zp_recv, pj_send, pj_recv, sm_send, sm_recv, pv_send, pv_recv,
    r1_send, r1_recv, r3_send, r3_recv,
):
    rows, cols, count, shard, tile, rank, strip = dims
    layers = rows // PLANE
    tiles = 2 * rows
    r = lax.axis_index("row")
    c = lax.axis_index("col")
    b = lax.rem(r, PLANE)
    a = lax.div(r, PLANE)
    x_at = lax.rem(r, 2)
    y_at = lax.div(b, 2)
    x_step = 1 - 2 * x_at
    y_step = 2 - 4 * y_at
    strips = shard // strip
    pending = []

    def remote(src, dst, send, recv, row, col):
        return pltpu.make_async_remote_copy(
            src_ref=src, dst_ref=dst, send_sem=send, recv_sem=recv,
            device_id=(row, col), device_id_type=MESH,
        )

    def push(*args):
        copy = remote(*args)
        copy.start()
        pending.append(copy)

    own_copies = {}
    off_copies = {}
    for h in range(2):
        for s in range(strips):
            width = (s + 1) * strip
            own_copies[h, s] = pltpu.make_async_copy(
                diag_ref.at[h, pl.ds(s * strip, strip), pl.ds(pl.multiple_of(c * shard, LANES), width)],
                down.at[h, pl.ds(s * strip, strip), pl.ds(0, width)],
                own_sem.at[h, s],
            )
            own_copies[h, s].start()
    for h in range(2):
        for d in range(1, cols):
            at = jnp.maximum(c - d, 0)
            off_copies[h, d] = pltpu.make_async_copy(
                diag_ref.at[h, :, pl.ds(pl.multiple_of(at * shard, LANES), shard)],
                doff.at[h, d - 1],
                off_sem.at[h, d - 1],
            )

            @pl.when(c >= d)
            def _(copy=off_copies[h, d]):
                copy.start()

    v_parts = v_sem.shape[0]
    part = tiles * rank // v_parts
    v_copies = [
        pltpu.make_async_copy(right_ref.at[pl.ds(i * part, part)], vbuf.at[pl.ds(i * part, part)], v_sem.at[i])
        for i in range(v_parts)
    ]
    u_copies = [
        pltpu.make_async_copy(left_ref.at[pl.ds(i * part, part)], ubuf.at[pl.ds(i * part, part)], u_sem.at[i])
        for i in range(v_parts)
    ]
    for copy in v_copies + u_copies:
        copy.start()

    for h in range(2):
        z_ref[h] = noise_ref[...].astype(jnp.float32)[:, h].astype(jnp.bfloat16)

    barrier = pltpu.get_barrier_semaphore()

    def greet(row, col):
        pl.semaphore_signal(barrier, inc=1, device_id=(row, col), device_id_type=MESH)

    col_peers = [lax.rem(c + d, cols) for d in range(1, cols)]
    place = b * cols + c
    block_slots = [lax.rem(place + d, PLANE * cols) for d in range(1, PLANE * cols)]
    block_peers = [(a * PLANE + lax.div(m, cols), lax.rem(m, cols), m) for m in block_slots]
    layer_peers = [lax.rem(a + d, layers) * PLANE + b for d in range(1, layers)]
    for row, col, slot in block_peers:
        greet(row, col)

    for peer in layer_peers:
        greet(peer, c)

    @pl.when(r < rows - 1)
    def _():
        for k in range(cols):
            greet(r + 1, k)

    @pl.when(r > 0)
    def _():
        for k in range(cols):
            greet(r - 1, k)

    expected = PLANE * cols - 1 + layers - 1
    expected = expected + jnp.where(r < rows - 1, cols, 0) + jnp.where(r > 0, cols, 0)
    pl.semaphore_wait(barrier, expected)

    def tile_of(owner, h):
        return owner if h == 0 else tiles - 1 - owner

    send_at = [0]
    guarded = []

    def z_push(src, owner, h, row, cond=None):
        j = tile_of(owner, h)
        copy = remote(src, zbuf.at[j], z_send.at[send_at[0]], z_recv.at[j], row, c)
        send_at[0] += 1
        if cond is None:
            copy.start()
            pending.append(copy)
        else:
            guarded.append((cond, copy))
            pl.when(cond)(copy.start)

    def z_wait(owner, h, cond=None):
        j = tile_of(owner, h)
        copy = remote(zbuf.at[j], zbuf.at[j], z_send.at[0], z_recv.at[j], r, c)
        if cond is None:
            copy.wait_recv()
        else:
            pl.when(cond)(copy.wait_recv)

    row_x = r + x_step
    row_y = r + y_step
    near = (row_y, row_x)
    far = (row_x, row_y)
    others = []
    for d in range(1, layers):
        other = lax.rem(a + jnp.where(2 * a < layers, d, layers - d), layers)
        others.append((other, other * PLANE + b))
    for other, peer in others:
        z_push(z_ref.at[0], r, 0, peer)
        z_push(z_ref.at[1], r, 1, peer, other < a)
    for h in range(2):
        z_push(z_ref.at[h], r, h, near[h])
        z_push(z_ref.at[h], r, h, far[h])
    for i, peer in enumerate(col_peers):
        push(z_ref, zpeer.at[c], zp_send.at[i], zp_recv.at[c], r, peer)
    for h in range(2):
        zbuf[tile_of(r, h)] = z_ref[h]

    def diag_chunk(h, s):
        own_copies[h, s].wait()
        lanes = pl.ds(s * strip, strip)
        block = down[h, lanes, lanes]
        below = (
            lax.broadcasted_iota(jnp.int32, (strip, strip), 1)
            < lax.broadcasted_iota(jnp.int32, (strip, strip), 0)
        )
        block = jnp.where(below, block.astype(jnp.float32), 0.0).astype(jnp.bfloat16)
        mine = z_ref[h, :, lanes]
        value = mine.astype(jnp.float32)
        value += lax.dot_general(mine, block, NT_DIMS, preferred_element_type=jnp.float32)
        if s:
            value += lax.dot_general(
                z_ref[h, :, : s * strip], down[h, lanes, : s * strip], NT_DIMS,
                preferred_element_type=jnp.float32,
            )
        acc[h * count : (h + 1) * count, lanes] = value

    def off_chunk(h, d):
        @pl.when(c >= d)
        def _():
            off_copies[h, d].wait()
            at = jnp.maximum(c - d, 0)
            acc[h * count : (h + 1) * count, :] += lax.dot_general(
                zpeer[at, h], doff[h, d - 1], NT_DIMS, preferred_element_type=jnp.float32
            )

    work = [functools.partial(diag_chunk, h, s) for h in range(2) for s in range(strips)]
    spare = [functools.partial(off_chunk, h, d) for h in range(2) for d in range(1, cols)]

    def some(n):
        for _ in range(n):
            if work:
                work.pop(0)()

    some(2)
    offsets = [(owner, (None, other > a)) for other, owner in others]
    for owner, there in offsets:
        for h in range(2):
            j = tile_of(owner, h)
            z_wait(owner, h, there[h])
            z_push(zbuf.at[j], owner, h, near[h], there[h])
            z_push(zbuf.at[j], owner, h, far[h], there[h])
        some(1)
    second_step = (y_step, x_step)
    for owner, there in [(r, (None, None))] + offsets:
        for h in range(2):
            from_near = owner + second_step[h]
            z_wait(from_near, h, there[h])
            j = tile_of(from_near, h)
            z_push(zbuf.at[j], from_near, h, far[h], there[h])
        some(1)
    some(len(work))
    for i, peer in enumerate(col_peers):
        remote(z_ref, zpeer.at[peer], zp_send.at[i], zp_recv.at[peer], r, peer).wait_recv()
    while spare:
        spare.pop(0)()
    last_step = (x_step, y_step)
    for owner, there in [(r, (None, None))] + offsets:
        for h in range(2):
            z_wait(owner + last_step[h], h, there[h])
            z_wait(owner + x_step + y_step, h, there[h])

    group = 256 // rank
    lane_slot = lax.div(lax.broadcasted_iota(jnp.int32, (count, group * rank), 1), rank)
    lane_rank = lax.rem(lax.broadcasted_iota(jnp.int32, (count, group * rank), 1), rank)
    waited = 0
    for g in range(tiles // group):
        while waited * part < (g + 1) * group * rank:
            v_copies[waited].wait()
            waited += 1
        chosen = []
        for i in range(group):
            k = g * group + i
            chosen.append(zbuf[jnp.where(k < r, k, jnp.maximum(k - r, 0))].astype(jnp.float32))
        lhs = jnp.concatenate(chosen, axis=0).astype(jnp.bfloat16)
        span = pl.ds(g * group * rank, group * rank)
        result = lax.dot_general(lhs, vbuf[span, :], NT_DIMS, preferred_element_type=jnp.float32)
        value = result[:count]
        for i in range(1, group):
            value = jnp.where(lane_slot == i, result[i * count : (i + 1) * count], value)
        proj[c, :, span] = value
    for i, peer in enumerate(col_peers):
        push(proj.at[c], proj.at[c], pj_send.at[i], pj_recv.at[c], r, peer)
    for copy in u_copies:
        copy.wait()
    for i, peer in enumerate(col_peers):
        remote(proj.at[c], proj.at[peer], pj_send.at[i], pj_recv.at[peer], r, peer).wait_recv()
    weighted = []
    for g in range(tiles // group):
        span = pl.ds(g * group * rank, group * rank)
        value = proj[0, :, span]
        for k in range(1, cols):
            value = value + proj[k, :, span]
        limit = jnp.zeros((count, group * rank), jnp.int32)
        for i in range(group):
            limit = jnp.where(lane_slot == i, ranks_ref[0, g * group + i], limit)
        value = jnp.where(lane_rank < limit, value, 0.0)
        slot = lane_slot + g * group
        weighted.append(
            jnp.concatenate(
                [
                    jnp.where(slot < r, value, 0.0),
                    jnp.where((slot >= r) & (slot < tiles - 1), value, 0.0),
                ],
                axis=0,
            ).astype(jnp.bfloat16)
        )
    weights = jnp.concatenate(weighted, axis=1)
    value = acc[...] + jnp.dot(weights, ubuf[...], preferred_element_type=jnp.float32)
    full[c] = value
    sbf[...] = value.astype(jnp.bfloat16)
    for i, peer in enumerate(col_peers):
        push(full.at[c], full.at[c], sm_send.at[i], sm_recv.at[c], r, peer)
    prev_copies = [
        remote(sbf, prev.at[c], pv_send.at[k], pv_recv.at[c], jnp.minimum(r + 1, rows - 1), k)
        for k in range(cols)
    ]

    @pl.when(r < rows - 1)
    def _():
        for copy in prev_copies:
            copy.start()

    for h in range(2):
        samples_ref[:, h, 0, :] = value[h * count : (h + 1) * count]
    groups = first_ref.shape[0]
    per_row = shard // LANES
    own_first = 2 * tile // LANES
    batch = 4

    def table(ref, h, j):
        return ref[j // per_row, h * count : (h + 1) * count, (j % per_row) * LANES : (j % per_row + 1) * LANES]

    def split(ref, at):
        index = jnp.broadcast_to(ref[pl.ds(at, 1), :], (count, LANES))
        return lax.shift_right_logical(index, 7), lax.bitwise_and(index, LANES - 1)

    def pick(entry, low):
        return jnp.take_along_axis(entry, low, axis=1, mode="promise_in_bounds")

    def own_part(k, fresh, step, carry):
        ats = [step * batch + i for i in range(batch)]
        base = own_first + k * per_row
        got = [[], []]
        for which, ref in enumerate((first_ref, second_ref)):
            for at in ats:
                high, low = split(ref, at)
                high = high - base
                value = jnp.zeros((count, LANES), jnp.float32)
                for h in range(2):
                    for j in range(per_row):
                        entry = full[k, h * count : (h + 1) * count, j * LANES : (j + 1) * LANES]
                        value = jnp.where(high == h * (tile // LANES) + j, pick(entry, low), value)
                got[which].append(value)
        for i in range(batch):
            value = got[0][i] - got[1][i]
            diff[ats[i]] = value if fresh else diff[ats[i]] + value
        return carry

    lax.fori_loop(0, groups // batch, functools.partial(own_part, c, True), 0)
    for i, peer in enumerate(col_peers):
        remote(full.at[c], full.at[peer], sm_send.at[i], sm_recv.at[peer], r, peer).wait_recv()
        lax.fori_loop(0, groups // batch, functools.partial(own_part, peer, False), 0)

    @pl.when(r > 0)
    def _():
        for k in range(cols):
            remote(sbf, prev.at[k], pv_send.at[k], pv_recv.at[k], r, c).wait_recv()
        prev32[...] = prev[...].astype(jnp.float32)

    @pl.when(r == 0)
    def _():
        prev32[...] = jnp.zeros_like(prev32)

    bin_rows = lax.broadcasted_iota(jnp.int32, (NBIN, LANES), 0)

    def prev_part(step, sums):
        ats = [step * batch + i for i in range(batch)]
        two = [split(second_ref, at) for at in ats]
        got = [jnp.zeros((count, LANES), jnp.float32) for _ in ats]
        for i in range(batch):
            for h in range(2):
                for j in range(tile // LANES):
                    entry = table(prev32, h, j)
                    number = h * (tile // LANES) + j
                    got[i] = jnp.where(two[i][0] == number, pick(entry, two[i][1]), got[i])
        for i in range(batch):
            differ = diff[ats[i]] - got[i]
            half_sq = 0.5 * differ * differ
            high = half_sq.astype(jnp.bfloat16).astype(jnp.float32)
            terms = jnp.concatenate(
                [high, half_sq - high, jnp.ones((count, LANES), jnp.float32)], axis=0
            ).astype(jnp.bfloat16)
            onehot = jnp.where(
                jnp.broadcast_to(bins_ref[pl.ds(ats[i], 1), :], (NBIN, LANES)) == bin_rows, 1.0, 0.0
            ).astype(jnp.bfloat16)
            sums = sums + lax.dot_general(terms, onehot, NT_DIMS, preferred_element_type=jnp.float32)
        return sums

    sums = lax.fori_loop(0, groups // batch, prev_part, jnp.zeros((3 * count, NBIN), jnp.float32))
    total = jnp.concatenate([sums[:count] + sums[count : 2 * count], sums[2 * count :]], axis=0)

    def reduce_stage(value, buf, at, peers, send, recv, number):
        buf[at] = value
        for i, (row, col, slot) in enumerate(peers):
            push(buf.at[at], buf.at[at], send.at[i], recv.at[at], row, col)
        for i, (row, col, slot) in enumerate(peers):
            remote(buf.at[at], buf.at[slot], send.at[i], recv.at[slot], row, col).wait_recv()
        out = buf[0]
        for i in range(1, number):
            out = out + buf[i]
        return out

    total = reduce_stage(total, red1, place, block_peers, r1_send, r1_recv, PLANE * cols)
    total = reduce_stage(
        total, red3, a, [(p, c, lax.div(p, PLANE)) for p in layer_peers], r3_send, r3_recv, layers
    )
    vario_ref[...] = total[:count] / jnp.maximum(total[count:], 1.0)

    for copy in pending:
        copy.wait_send()
    for cond, copy in guarded:
        pl.when(cond)(copy.wait_send)

    @pl.when(r < rows - 1)
    def _():
        for copy in prev_copies:
            copy.wait_send()


def body(
    noise, diag_factor, left_factor, right_factor, tile_ranks, pair_first, pair_partner, bin_ids
):
    rows = lax.axis_size("row")
    cols = lax.axis_size("col")
    count = noise.shape[0]
    shard = noise.shape[3]
    tile = shard * cols
    tiles = 2 * rows
    rank = right_factor.shape[2]
    strip = min(256, shard)
    layers = rows // PLANE
    v_parts = 4
    dma = lambda *shape: pltpu.SemaphoreType.DMA(shape)
    vmem = pl.BlockSpec(memory_space=pltpu.VMEM)
    hbm = pl.BlockSpec(memory_space=pl.ANY)
    smem = pl.BlockSpec(memory_space=pltpu.SMEM)
    off = max(cols - 1, 1)
    f32, bf16 = jnp.float32, jnp.bfloat16
    samples, vario = pl.pallas_call(
        functools.partial(kernel, (rows, cols, count, shard, tile, rank, strip)),
        out_shape=(
            jax.ShapeDtypeStruct((count, 2, 1, shard), f32),
            jax.ShapeDtypeStruct((count, NBIN), f32),
        ),
        in_specs=[vmem, hbm, hbm, hbm, smem, vmem, vmem, vmem],
        out_specs=(vmem, vmem),
        scratch_shapes=[
            pltpu.VMEM((2, count, shard), bf16),
            pltpu.VMEM((tiles, count, shard), bf16),
            pltpu.VMEM((cols, 2, count, shard), bf16),
            pltpu.VMEM((2, shard, shard), bf16),
            pltpu.VMEM((2, off, shard, shard), bf16),
            pltpu.VMEM((tiles * rank, shard), bf16),
            pltpu.VMEM((tiles * rank, shard), bf16),
            pltpu.VMEM((cols, count, tiles * rank), f32),
            pltpu.VMEM((2 * count, shard), f32),
            pltpu.VMEM((cols, 2 * count, shard), f32),
            pltpu.VMEM((2 * count, shard), bf16),
            pltpu.VMEM((cols, 2 * count, shard), bf16),
            pltpu.VMEM((cols, 2 * count, shard), f32),
            pltpu.VMEM((pair_first.shape[2] // LANES, count, LANES), f32),
            pltpu.VMEM((PLANE * cols, 2 * count, NBIN), f32),
            pltpu.VMEM((layers, 2 * count, NBIN), f32),
            dma(2, shard // strip), dma(2, off), dma(v_parts), dma(v_parts),
            dma(16 * layers), dma(tiles), dma(off), dma(cols),
            dma(off), dma(cols), dma(off), dma(cols), dma(cols), dma(cols),
            dma(PLANE * cols), dma(PLANE * cols), dma(layers), dma(layers),
        ],
        compiler_params=pltpu.CompilerParams(collective_id=0, has_side_effects=True),
    )(
        noise.reshape(count, 2, shard),
        diag_factor.reshape(2, shard, tile),
        left_factor.reshape(tiles * rank, shard),
        right_factor.reshape(tiles * rank, shard),
        tile_ranks,
        pair_first.reshape(-1, LANES),
        pair_partner.reshape(-1, LANES),
        bin_ids.reshape(-1, LANES),
    )
    return samples, vario


def solution(mesh):
    in_specs = (
        P(None, None, "row", "col"),
        P(None, "row", "col", None),
        P("row", None, None, "col"),
        P("row", None, None, "col"),
        P("row", None),
        P("row", "col", None),
        P("row", "col", None),
        P("row", "col", None),
    )
    out_specs = (P(None, None, "row", "col"), P())
    return jax.shard_map(body, mesh=mesh, in_specs=in_specs, out_specs=out_specs, check_vma=False)
```
